256 devices in a mesh: rows: 32 (over z, y), cols: 8 (over x, core).
Axes of the slice: x: 4, y: 4, z: 8, core: 2. Of those that a mesh axis runs over, the one named last changes fastest.
Arguments:
- points: bfloat16 [131072, 128], P(('rows', 'cols')), may hold values from -6 to 6
- gradient: float32 [131072, 128], P(('rows', 'cols')), may hold values from -6 to 6
- panel_index: int32 [16, 1024], P('cols'), may hold values from 0 to 131071, as said below
Outputs:
- new_gradient: float32 [131072, 128], P(('rows', 'cols'))
- update: float32 [16384, 128], P('cols')
The draws below stay inside these ranges and needn't reach their ends.
Inputs may be any that keep to these rules, and one draw needn't show every extreme that they name: `panel_index`: all 16384 indices are distinct.
All inputs are finite; a program needn't handle non-finite values.
Results may differ from the reference program's by a relative error of at most 0.0015.
The reference program's roundings to bfloat16 on the way (of `chosen`, `update_half` and `tile`) count: a program that leaves them out, or rounds other values in their place, can miss the bound.
Values may be sent and summed in bfloat16 or wider, within the bound.
No kernel may reach another device: no remote copies, remote signals or barrier semaphores. Data moves between devices by JAX's collectives and lax.ppermute only.
A program may use at most 128 MiB of HBM per device.

```python
import math
import jax
import jax.numpy as jnp
from jax import lax

FEATURES = 128
TARGETS = 128
BLOCK = 1024
ITERS = 8
POINTS = 131072
BLOCKS = 16
PANEL = 16384


def draw_panel_index(key, part):
    first_key, second_key = jax.random.split(jax.random.fold_in(key, 17))
    shuffled = jax.random.permutation(first_key, POINTS).astype(jnp.int32)
    lowest_at = jnp.argmin(shuffled)
    shuffled = shuffled.at[lowest_at].set(shuffled[0])
    shuffled = shuffled.at[0].set(0)
    highest_at = jnp.argmax(shuffled)
    shuffled = shuffled.at[highest_at].set(shuffled[1])
    shuffled = shuffled.at[1].set(POINTS - 1)
    chosen = shuffled[:BLOCKS * BLOCK]
    chosen = jax.random.permutation(second_key, chosen)
    return chosen.reshape(BLOCKS, BLOCK).astype(jnp.int32)


def block_levels(own_key, dims, cuts, least, top_value):
    def one(position, blocks):
        heights = jax.random.uniform(jax.random.fold_in(jax.random.fold_in(own_key, 6), position), (blocks,), jnp.float32, least / len(cuts), top_value / len(cuts))
        return jnp.repeat(jnp.exp(heights), dims[position] // blocks).reshape((-1,) + (1,) * (len(dims) - position - 1))

    factor_of = one(*cuts[0])
    for cut in cuts[1:]:
        factor_of = factor_of * one(*cut)
    return factor_of


def noise(key, dims, deviation, most, pieces=(), held_as=jnp.bfloat16):
    result = jax.random.normal(key, dims, jnp.float32) * deviation
    if len(pieces) > 0:
        result = block_levels(key, dims, pieces, -0.22, 0.18) * result
    return jnp.clip(result, min=-most, max=most).astype(held_as)


def setup_inputs(seed: int = 0) -> dict:
    key_list = jax.random.split(jax.random.key(seed), 4)
    points = noise(key_list[0], (POINTS, FEATURES), 1.0, 6.0, ((0, 256),))
    gradient = noise(key_list[1], (POINTS, TARGETS), 1.0, 6.0, ((0, 256),), jnp.float32)
    panel_index = draw_panel_index(jax.random.fold_in(key_list[3], 71), 0)
    return {"points": points, "gradient": gradient, "panel_index": panel_index}


ridge_weight = 1.0


def kernel_tile(left_points, right_points):
    left_square = jnp.sum(jnp.square(left_points.astype(jnp.float32)), axis=-1)
    right_square = jnp.sum(jnp.square(right_points.astype(jnp.float32)), axis=-1)
    inner = jnp.dot(left_points, right_points.T, preferred_element_type=jnp.float32)
    distance = jnp.maximum(left_square[:, None] + right_square[None, :] - 2.0 * inner, 0.0)
    return jnp.exp(distance * (-2.0 / left_points.shape[-1]))


def chebyshev(matrix, right_side):
    upper = jnp.max(jnp.sum(matrix, axis=1))
    lower = ridge_weight
    center = (upper + lower) / 2.0
    radius = (upper - lower) / 2.0
    ratio = center / radius
    factor = 1.0 / ratio
    residual = right_side
    direction = residual / center
    solution = jnp.zeros_like(right_side)
    for iteration in range(ITERS):
        solution = solution + direction
        if iteration < ITERS - 1:
            residual = residual - jnp.dot(matrix, direction, precision=lax.Precision.HIGHEST)
            following = 1.0 / (2.0 * ratio - factor)
            direction = following * factor * direction + (2.0 * following / radius) * residual
            factor = following
    return solution


def reference(points, gradient, panel_index):
    indices = panel_index.reshape(-1)
    chosen = points[indices]
    chosen_gradient = gradient[indices]

    def solve_block(item):
        block_points, block_gradient = item
        matrix = kernel_tile(block_points, block_points) + ridge_weight * jnp.eye(BLOCK, dtype=jnp.float32)
        return chebyshev(matrix, -block_gradient)

    update = lax.map(solve_block, (chosen.reshape(BLOCKS, BLOCK, FEATURES), chosen_gradient.reshape(BLOCKS, BLOCK, TARGETS)))
    update = update.reshape(PANEL, TARGETS)
    update_half = update.astype(jnp.bfloat16)
    piece = math.gcd(POINTS, 512)

    def update_rows(start):
        block_points = lax.dynamic_slice_in_dim(points, start, piece, 0)
        row_ids = start + jnp.arange(piece, dtype=jnp.int32)
        tile = kernel_tile(block_points, chosen) + ridge_weight * (row_ids[:, None] == indices[None, :]).astype(jnp.float32)
        change = jnp.dot(tile.astype(jnp.bfloat16), update_half, preferred_element_type=jnp.float32)
        return lax.dynamic_slice_in_dim(gradient, start, piece, 0) + change

    starts = (jnp.arange(POINTS // piece) * piece).astype(jnp.int32)
    new_gradient = lax.map(update_rows, starts).reshape(POINTS, TARGETS)
    return new_gradient, update
```

```python
import functools

import jax
import jax.numpy as jnp
from jax import lax
from jax.experimental import pallas as pl
from jax.experimental.pallas import tpu as pltpu
from jax.sharding import Mesh
from jax.sharding import PartitionSpec as P

ITERS = 8
RIDGE = 1.0
LOG2E = 1.4426950408889634
ROWS = ("z", "y")
DEVICES = ("z", "y", "x", "k")
TRANSPOSED = (((1,), (1,)), ((), ()))


def solve_kernel(points_ref, column_ref, row_ref, right_ref, update_ref, high_ref, low_ref):
    width = points_ref.shape[0]
    scale = -2.0 / points_ref.shape[1] * LOG2E
    step = 256
    upper = jnp.zeros((1, 1), jnp.float32)
    for start in range(0, width, step):
        piece = pl.ds(start, step)
        inner = lax.dot_general(
            points_ref[piece, :], points_ref[...], TRANSPOSED, preferred_element_type=jnp.float32
        )
        distance = jnp.maximum(column_ref[piece, :] + row_ref[...] - 2.0 * inner, 0.0)
        values = jnp.exp2(distance * scale)
        sums = jnp.sum(values, axis=1, keepdims=True)
        upper = jnp.maximum(upper, jnp.max(sums, axis=0, keepdims=True))
        high = values.astype(jnp.bfloat16)
        high_ref[piece, :] = high
        low_ref[piece, :] = (values - high.astype(jnp.float32)).astype(jnp.bfloat16)
    upper = upper + RIDGE
    center = (upper + RIDGE) / 2.0
    radius = (upper - RIDGE) / 2.0
    ratio = center / radius
    factor = 1.0 / ratio
    residual = right_ref[...]
    targets = residual.shape[0]
    direction = residual / center
    update = jnp.zeros_like(residual)
    for iteration in range(ITERS):
        update = update + direction
        if iteration < ITERS - 1:
            high = direction.astype(jnp.bfloat16)
            low = (direction - high.astype(jnp.float32)).astype(jnp.bfloat16)
            both = jnp.concatenate([high, low], axis=0)
            main = jnp.dot(both, high_ref[...], preferred_element_type=jnp.float32)
            rest = jnp.dot(high, low_ref[...], preferred_element_type=jnp.float32)
            product = main[:targets] + (main[targets:] + rest)
            residual = residual - (product + RIDGE * direction)
            following = 1.0 / (2.0 * ratio - factor)
            direction = following * factor * direction + 2.0 * following / radius * residual
            factor = following
    update_ref[...] = update


def solve(points, right_side):
    width, _ = points.shape
    squares = jnp.sum(jnp.square(points.astype(jnp.float32)), axis=-1)
    return pl.pallas_call(
        solve_kernel,
        out_shape=jax.ShapeDtypeStruct(right_side.shape, jnp.float32),
        in_specs=[pl.BlockSpec(memory_space=pltpu.VMEM)] * 4,
        out_specs=pl.BlockSpec(memory_space=pltpu.VMEM),
        scratch_shapes=[pltpu.VMEM((width, width), jnp.bfloat16)] * 2,
        compiler_params=pltpu.CompilerParams(vmem_limit_bytes=40 << 20),
        name="solve",
    )(points, squares[:, None], squares[None, :], right_side)


def change_kernel(points_ref, column_ref, ids_ref, chosen_ref, row_ref, panel_ref, update_ref, out_ref):
    scale = -2.0 / points_ref.shape[1] * LOG2E
    step = 512
    total = jnp.zeros(out_ref.shape, jnp.float32)
    for start in range(0, chosen_ref.shape[0], step):
        piece = pl.ds(start, step)
        inner = lax.dot_general(
            points_ref[...], chosen_ref[piece, :], TRANSPOSED, preferred_element_type=jnp.float32
        )
        distance = jnp.maximum(column_ref[...] + row_ref[:, piece] - 2.0 * inner, 0.0)
        values = jnp.exp2(distance * scale)
        values = jnp.where(ids_ref[...] == panel_ref[:, piece], values + RIDGE, values)
        total = total + lax.dot_general(
            values.astype(jnp.bfloat16),
            update_ref[:, piece],
            TRANSPOSED,
            preferred_element_type=jnp.float32,
        )
    out_ref[...] = total


def change(points, ids, chosen, panel, update):
    count, features = points.shape
    width = chosen.shape[0]
    targets = update.shape[0]
    block = 256
    point_squares = jnp.sum(jnp.square(points.astype(jnp.float32)), axis=-1)
    panel_squares = jnp.sum(jnp.square(chosen.astype(jnp.float32)), axis=-1)
    return pl.pallas_call(
        change_kernel,
        grid=(count // block,),
        out_shape=jax.ShapeDtypeStruct((count, targets), jnp.float32),
        in_specs=[
            pl.BlockSpec((block, features), lambda i: (i, 0)),
            pl.BlockSpec((block, 1), lambda i: (i, 0)),
            pl.BlockSpec((block, 1), lambda i: (i, 0)),
            pl.BlockSpec((width, features), lambda i: (0, 0)),
            pl.BlockSpec((1, width), lambda i: (0, 0)),
            pl.BlockSpec((1, width), lambda i: (0, 0)),
            pl.BlockSpec((targets, width), lambda i: (0, 0)),
        ],
        out_specs=pl.BlockSpec((block, targets), lambda i: (i, 0)),
        compiler_params=pltpu.CompilerParams(vmem_limit_bytes=40 << 20),
        name="change",
    )(points, point_squares[:, None], ids[:, None], chosen, panel_squares[None, :], panel[None, :], update)


def spread(piece, axes):
    count = lax.axis_size(axes)
    return lax.all_to_all(jnp.broadcast_to(piece[None], (count, *piece.shape)), axes, 0, 0)


def on_device(points, gradient, panel_index):
    own, features = points.shape
    targets = gradient.shape[1]
    blocks, width = panel_index.shape
    xs, ks = lax.axis_size("x"), lax.axis_size("k")
    rows = lax.axis_size(ROWS)
    row = lax.axis_index(ROWS)
    core = lax.axis_index("k")
    group = own * xs * ks

    core_points = lax.all_gather(points, "x")
    row_points = lax.all_gather(core_points, "k", axis=1).reshape(group, features)
    core_grads = lax.all_gather(gradient, "x")
    row_grads = lax.all_gather(core_grads, "k", axis=1).reshape(group, targets)

    indices = panel_index.reshape(-1)
    offset = indices - row * group
    inside = ((offset >= 0) & (offset < group))[:, None]
    clipped = jnp.clip(offset, 0, group - 1)
    picked_points = jnp.where(inside, jnp.take(row_points, clipped, axis=0), jnp.zeros((), jnp.bfloat16))
    picked_grads = jnp.where(inside, jnp.take(row_grads, clipped, axis=0), 0.0)

    shard = blocks * width
    pieces = lax.all_to_all(picked_points.reshape(rows, shard // rows, features), ROWS, 0, 0)
    piece = jnp.sum(pieces.astype(jnp.float32), axis=0).astype(jnp.bfloat16)
    chosen = spread(piece, ROWS).reshape(shard, features)

    groups = rows // blocks
    slices = picked_grads.T.reshape(groups, targets // groups, blocks, width)
    slices = slices.transpose(0, 2, 1, 3).reshape(rows, targets // groups, width)
    right_side = -jnp.sum(lax.all_to_all(slices, ROWS, 0, 0), axis=0)

    own_block = lax.dynamic_index_in_dim(chosen.reshape(blocks, width, features), row % blocks, 0, False)
    solved = solve(own_block, right_side)
    half = spread(solved.astype(jnp.bfloat16), ROWS)
    half = half.reshape(groups, blocks, targets // groups, width).transpose(0, 2, 1, 3)
    half = half.reshape(targets, shard)

    both_chosen = lax.all_gather(chosen, "k", axis=0, tiled=True)
    both_panel = lax.all_gather(indices, "k", axis=0, tiled=True)
    both_half = lax.all_gather(half, "k", axis=1, tiled=True)
    ids = row * group + core * own
    ids = ids + ks * own * jnp.arange(xs, dtype=jnp.int32)[:, None] + jnp.arange(own, dtype=jnp.int32)[None, :]
    term = change(core_points.reshape(xs * own, features), ids.reshape(-1), both_chosen, both_panel, both_half)
    terms = lax.all_to_all(term.reshape(xs, own, targets), "x", 0, 0)
    new_gradient = gradient + jnp.sum(terms, axis=0)

    full = spread(solved, ROWS).reshape(groups, blocks, targets // groups, width)
    update = full.transpose(1, 3, 0, 2).reshape(shard, targets)
    return new_gradient, update


def solution(mesh):
    fine = Mesh(mesh.devices.reshape(8, 4, 4, 2), DEVICES)
    in_specs = (P(DEVICES, None), P(DEVICES, None), P(("x", "k"), None))
    out_specs = (P(DEVICES, None), P(("x", "k"), None))
    return jax.shard_map(on_device, mesh=fine, in_specs=in_specs, out_specs=out_specs, check_vma=False)
```

```python
import jax
import jax.numpy as jnp
from jax import lax
from jax.experimental import pallas as pl
from jax.experimental.pallas import tpu as pltpu
from jax.sharding import Mesh
from jax.sharding import PartitionSpec as P

ITERS = 8
RIDGE = 1.0
LOG2E = 1.4426950408889634
DEVICES = ("z", "y", "x", "k")
ROUTE = ("x", "z", "y")
ROWS = ("z", "y")
TRANSPOSED = (((1,), (1,)), ((), ()))
FIRST = (((0,), (0,)), ((), ()))
MIB = 1 << 20
POINT_SLOTS = 10
GRAD_SLOTS = 32
SLOTS = 16
FEW = 8
CHIPS = 128
XS = 4
OWN = 1024
NONE = 1 << 20


def iota(shape, axis):
    return lax.broadcasted_iota(jnp.int32, shape, axis)


def owner_place(index, own, xs, rows):
    chip = index // own
    return (chip % xs) * rows + chip // xs


def pack_kernel(
    scalar_ref, here_ref, one_ref, two_ref, three_ref, points_ref, other_points_ref, grads_ref, other_grads_ref,
    out_ref, values_ref, rows_ref, table_ref,
):
    tables = (here_ref, one_ref, two_ref, three_ref)
    per_shard, width = here_ref.shape
    each, targets = grads_ref.shape
    own = 2 * each
    groups = targets // FEW
    blocks = len(tables) * per_shard
    devices = blocks * groups
    share = width // groups
    per = 128 // FEW
    number = scalar_ref[0]
    for back, table in enumerate(tables):
        shard = (scalar_ref[2] - back) & (len(tables) - 1)
        for lane in range(0, width, 128):
            pair = table[:, lane : lane + 128]
            turned = pltpu.roll(pair, share, 1)
            for block in range(per_shard):
                line = (shard * per_shard + block) * groups + lane // share
                table_ref[pl.ds(line, 1), :] = pair[block : block + 1]
                table_ref[pl.ds(line + 1, 1), :] = turned[block : block + 1]
    offset = table_ref[:, :share] - scalar_ref[1]
    mine = (offset >= 0) & (offset < own)
    held = mine.astype(jnp.bfloat16)
    offset = jnp.where(scalar_ref[3] == 0, offset, jnp.where(offset < each, offset + each, offset - each))
    code = jnp.where(mine, (offset + 1).astype(jnp.float32), 0.0)
    upper = (iota((share, share), 0) < iota((share, share), 1)).astype(jnp.bfloat16)
    rank = jnp.dot(held, upper, preferred_element_type=jnp.float32)
    count = jnp.dot(held, jnp.ones((share, share), jnp.bfloat16), preferred_element_type=jnp.float32)
    left, right = iota((devices, devices), 0), iota((devices, devices), 1)
    earlier = ((left // groups == right // groups) & (right < left)).astype(jnp.bfloat16)
    before = jnp.dot(earlier, count.astype(jnp.bfloat16), preferred_element_type=jnp.float32)
    block_rank = rank + before

    lanes = iota((devices, own), 1)
    first = (number * POINT_SLOTS).astype(jnp.float32)
    for slot in range(POINT_SLOTS):
        chosen = jnp.sum(jnp.where(rank == first + slot, code, 0.0), axis=1, keepdims=True)
        pick = (lanes + 1 == chosen.astype(jnp.int32)).astype(jnp.bfloat16)
        rows_ref[pl.ds(slot, devices, stride=SLOTS), :] = jnp.dot(
            pick[:, :each], points_ref[...], preferred_element_type=jnp.float32
        ) + jnp.dot(pick[:, each:], other_points_ref[...], preferred_element_type=jnp.float32)

    lanes = iota((devices, 128), 1)
    keep = iota((blocks, 128), 1) // per == iota((blocks, 128), 0)
    parts = []
    left = jnp.concatenate([grads_ref[...], other_grads_ref[...]], axis=0)
    for _ in range(3):
        part = left.astype(jnp.bfloat16)
        left = left - part.astype(jnp.float32)
        parts.append(part)
    for turn in range(GRAD_SLOTS // per):
        first = (number * GRAD_SLOTS + turn * per).astype(jnp.float32)
        found = jnp.zeros((devices, 128), jnp.float32)
        for slot in range(per):
            chosen = jnp.sum(jnp.where(block_rank == first + slot, code, 0.0), axis=1, keepdims=True)
            found = jnp.where(lanes % per == slot, chosen, found)
        found = jnp.sum(found.reshape(blocks, groups, 128), axis=1)
        found = jnp.sum(jnp.where(keep, found, 0.0), axis=0, keepdims=True).astype(jnp.int32)
        pick = (iota((own, 128), 0) + 1 == found).astype(jnp.bfloat16)
        values = jnp.zeros((targets, 128), jnp.float32)
        for part in parts:
            values = values + lax.dot_general(part, pick, FIRST, preferred_element_type=jnp.float32)
        values_ref[...] = values
        places = iota((groups, 128), 1) // per
        message = [jnp.zeros((groups, 128), jnp.float32) for _ in range(blocks)]
        for target in range(FEW):
            taken = values_ref[pl.ds(target, groups, stride=FEW), :]
            for block in range(blocks):
                by = (target - block) * per % 128
                turned = pltpu.roll(taken, by, 1) if by else taken
                message[block] = jnp.where(places == target, turned, message[block])
        left = jnp.concatenate(message, axis=0)
        for place in range(3):
            part = left.astype(jnp.bfloat16).astype(jnp.float32)
            left = left - part
            rows_ref[pl.ds(POINT_SLOTS + 3 * turn + place, devices, stride=SLOTS), :] = part
    out_ref[...] = rows_ref[...].astype(jnp.bfloat16)


def pack(scalars, tables, points, other_points, grads, other_grads):
    targets = grads.shape[1]
    devices = len(tables) * tables[0].shape[0] * targets // FEW
    vmem = pl.BlockSpec(memory_space=pltpu.VMEM)
    return pl.pallas_call(
        pack_kernel,
        out_shape=jax.ShapeDtypeStruct((devices * SLOTS, 128), jnp.bfloat16),
        in_specs=[pl.BlockSpec(memory_space=pltpu.SMEM)] + [vmem] * 8,
        out_specs=vmem,
        scratch_shapes=[
            pltpu.VMEM((targets, 128), jnp.float32),
            pltpu.VMEM((devices * SLOTS, 128), jnp.float32),
            pltpu.VMEM((devices, 128), jnp.int32),
        ],
        compiler_params=pltpu.CompilerParams(vmem_limit_bytes=16 * MIB),
        name="pack",
    )(scalars, *tables, points, other_points, grads, other_grads)


def ranks_kernel(here_ref, one_ref, two_ref, three_ref, block_row_ref, block_column_ref, rounds_ref, rank_ref):
    tables = (here_ref, one_ref, two_ref, three_ref)
    per_shard, width = here_ref.shape
    share = width // 16
    segments = iota((width, 128), 0) // share == iota((width, 128), 1)
    segments = segments | (iota((width, 128), 1) == 127)
    segments = segments.astype(jnp.bfloat16)
    most = jnp.zeros((CHIPS, 128), jnp.float32)
    chip = iota((CHIPS, width), 0)

    def count(block, most):
        for table in tables:
            hit = (chip == table[pl.ds(block, 1), :] // OWN).astype(jnp.bfloat16)
            most = jnp.maximum(most, jnp.dot(hit, segments, preferred_element_type=jnp.float32))
        return most

    most = lax.fori_loop(0, per_shard, count, most)
    whole = iota((CHIPS, 128), 1) == 127
    most_block = jnp.max(jnp.where(whole, most, 0.0), keepdims=True).astype(jnp.int32)
    most_share = jnp.max(jnp.where(whole, 0.0, most), keepdims=True).astype(jnp.int32)
    rounds_ref[...] = jnp.maximum(
        (most_block + GRAD_SLOTS - 1) // GRAD_SLOTS, (most_share + POINT_SLOTS - 1) // POINT_SLOTS
    )
    owners = block_row_ref[...] // OWN
    step = 128

    def compare(number, total):
        start = pl.multiple_of(number * step, step)
        others = block_column_ref[pl.ds(start, step), :] // OWN
        earlier = iota((step, width), 0) + start < iota((step, width), 1)
        same = jnp.where((others == owners) & earlier, 1, 0)
        return total + jnp.sum(same.reshape(step // 8, 8, width), axis=0)

    total = lax.fori_loop(0, width // step, compare, jnp.zeros((8, width), jnp.int32))
    rank_ref[...] = jnp.sum(total, axis=0, keepdims=True)


def ranks(tables, block_index):
    vmem = pl.BlockSpec(memory_space=pltpu.VMEM)
    width = block_index.shape[0]
    return pl.pallas_call(
        ranks_kernel,
        out_shape=(
            jax.ShapeDtypeStruct((1, 1), jnp.int32),
            jax.ShapeDtypeStruct((1, width), jnp.int32),
        ),
        in_specs=[vmem] * 6,
        out_specs=(vmem, vmem),
        compiler_params=pltpu.CompilerParams(vmem_limit_bytes=16 * MIB),
        cost_estimate=pl.CostEstimate(flops=4 * 10**9, bytes_accessed=10**5, transcendentals=0),
        name="ranks",
    )(*tables, block_index[None, :], block_index[:, None])


def place_kernel(scalar_ref, message_ref, row_ref, column_ref, block_ref, rank_ref, piece_ref, right_ref):
    length = message_ref.shape[0]
    share = column_ref.shape[0]
    width = block_ref.shape[1]
    per = 128 // FEW
    turns = GRAD_SLOTS // per
    number = scalar_ref[0]
    row_owner = owner_place(row_ref[...], OWN, XS, CHIPS // XS)
    column_owner = owner_place(column_ref[...], OWN, XS, CHIPS // XS)
    earlier = iota((share, share), 1) < iota((share, share), 0)
    rank = jnp.sum(
        jnp.where((row_owner == column_owner) & earlier, 1.0, 0.0), axis=1, keepdims=True
    ).astype(jnp.int32)
    slot = rank - number * POINT_SLOTS
    code = jnp.where((slot >= 0) & (slot < POINT_SLOTS), column_owner * SLOTS + slot, -1)
    pick = (iota((share, length), 1) == code).astype(jnp.bfloat16)
    piece = jnp.dot(pick, message_ref[...], preferred_element_type=jnp.float32).astype(jnp.bfloat16)
    for copy in range(piece_ref.shape[0]):
        piece_ref[copy] = piece

    slot = rank_ref[...] - number * GRAD_SLOTS
    wanted = owner_place(block_ref[...], OWN, XS, CHIPS // XS) * turns + slot // per
    wanted = jnp.where((slot >= 0) & (slot < GRAD_SLOTS), wanted, -NONE)
    step = 256
    def gather(number, found):
        start = pl.multiple_of(number * step, step)
        line = iota((step, width), 0)
        turn = (line % SLOTS - POINT_SLOTS + 3) // 3 - 1
        source = jnp.where((turn >= 0) & (turn < turns), line // SLOTS * turns + turn, 2 * NONE)
        pick = (source == wanted - number * (step // SLOTS * turns)).astype(jnp.bfloat16)
        return found + lax.dot_general(
            message_ref[pl.ds(start, step), :], pick, FIRST, preferred_element_type=jnp.float32
        )

    found = lax.fori_loop(0, length // step, gather, jnp.zeros((128, width), jnp.float32), unroll=2)
    here = iota((per, width), 0) == slot % per
    for target in range(FEW):
        part = found[target * per : (target + 1) * per]
        right_ref[pl.ds(target, 1), :] = -jnp.sum(jnp.where(here, part, 0.0), axis=0, keepdims=True)


def place(scalars, message, index, block_index, rank, copies):
    vmem = pl.BlockSpec(memory_space=pltpu.VMEM)
    share, width = index.shape[0], block_index.shape[0]
    return pl.pallas_call(
        place_kernel,
        out_shape=(
            jax.ShapeDtypeStruct((copies, share, 128), jnp.bfloat16),
            jax.ShapeDtypeStruct((FEW, width), jnp.float32),
        ),
        in_specs=[pl.BlockSpec(memory_space=pltpu.SMEM)] + [vmem] * 5,
        out_specs=(vmem, vmem),
        compiler_params=pltpu.CompilerParams(vmem_limit_bytes=16 * MIB),
        name="place",
    )(scalars, message, index[None, :], index[:, None], block_index[None, :], rank)


def solve_kernel(points_ref, right_ref, half_ref, rest_ref, high_ref, low_ref):
    width = points_ref.shape[0]
    scale = -2.0 / points_ref.shape[1] * LOG2E
    step = 256
    same = iota((step, step), 0) == iota((step, step), 1)
    columns, lines = [], []
    for start in range(0, width, step):
        part = points_ref[pl.ds(start, step), :]
        inner = lax.dot_general(part, part, TRANSPOSED, preferred_element_type=jnp.float32)
        inner = jnp.where(same, inner, 0.0)
        columns.append(jnp.sum(inner, axis=1, keepdims=True))
        lines.append(jnp.sum(inner, axis=0, keepdims=True))
    line = jnp.concatenate(lines, axis=1)
    upper = jnp.zeros((1, 1), jnp.float32)
    for number, start in enumerate(range(0, width, step)):
        piece = pl.ds(start, step)
        inner = lax.dot_general(
            points_ref[piece, :], points_ref[...], TRANSPOSED, preferred_element_type=jnp.float32
        )
        distance = jnp.maximum(columns[number] + line - 2.0 * inner, 0.0)
        values = jnp.exp2(distance * scale)
        sums = jnp.sum(values, axis=1, keepdims=True)
        upper = jnp.maximum(upper, jnp.max(sums, axis=0, keepdims=True))
        high = values.astype(jnp.bfloat16)
        high_ref[piece, :] = high
        low_ref[piece, :] = (values - high.astype(jnp.float32)).astype(jnp.bfloat16)
    upper = upper + RIDGE
    center = (upper + RIDGE) / 2.0
    radius = (upper - RIDGE) / 2.0
    ratio = center / radius
    factor = 1.0 / ratio
    residual = right_ref[...]
    targets = residual.shape[0]
    direction = residual / center
    update = jnp.zeros_like(residual)
    for iteration in range(ITERS):
        update = update + direction
        if iteration < ITERS - 1:
            high = direction.astype(jnp.bfloat16)
            low = (direction - high.astype(jnp.float32)).astype(jnp.bfloat16)
            both = jnp.concatenate([high, low], axis=0)
            main = jnp.dot(both, high_ref[...], preferred_element_type=jnp.float32)
            rest = jnp.dot(high, low_ref[...], preferred_element_type=jnp.float32)
            product = main[:targets] + (main[targets:] + rest)
            residual = residual - (product + RIDGE * direction)
            following = 1.0 / (2.0 * ratio - factor)
            direction = following * factor * direction + 2.0 * following / radius * residual
            factor = following
    half = update.astype(jnp.bfloat16)
    rest = (update - half.astype(jnp.float32)).astype(jnp.bfloat16)
    for copy in range(half_ref.shape[0]):
        half_ref[copy] = half
        rest_ref[copy] = rest


def solve(points, right_side, copies):
    width, _ = points.shape
    vmem = pl.BlockSpec(memory_space=pltpu.VMEM)
    return pl.pallas_call(
        solve_kernel,
        out_shape=(jax.ShapeDtypeStruct((copies, *right_side.shape), jnp.bfloat16),) * 2,
        in_specs=[vmem] * 2,
        out_specs=(vmem, vmem),
        scratch_shapes=[pltpu.VMEM((width, width), jnp.bfloat16)] * 2,
        compiler_params=pltpu.CompilerParams(vmem_limit_bytes=16 * MIB),
        cost_estimate=pl.CostEstimate(flops=6 * 10**9, bytes_accessed=10**6, transcendentals=width * width),
        name="solve",
    )(points, right_side)


def tile_kernel(points_ref, column_ref, ids_ref, chosen_ref, row_ref, panel_ref, out_ref):
    scale = -2.0 / points_ref.shape[1] * LOG2E
    step = 512
    for start in range(0, chosen_ref.shape[0], step):
        piece = pl.ds(start, step)
        inner = lax.dot_general(
            points_ref[...], chosen_ref[piece, :], TRANSPOSED, preferred_element_type=jnp.float32
        )
        distance = jnp.maximum(column_ref[...] + row_ref[:, piece] - 2.0 * inner, 0.0)
        values = jnp.exp2(distance * scale)
        values = jnp.where(ids_ref[...] == panel_ref[:, piece], values + RIDGE, values)
        out_ref[:, piece] = values.astype(jnp.bfloat16)


def build_tile(points, ids, chosen, panel):
    count, features = points.shape
    width = chosen.shape[0]
    block = 256
    point_squares = jnp.sum(jnp.square(points.astype(jnp.float32)), axis=-1)
    panel_squares = jnp.sum(jnp.square(chosen.astype(jnp.float32)), axis=-1)
    return pl.pallas_call(
        tile_kernel,
        grid=(count // block,),
        out_shape=jax.ShapeDtypeStruct((count, width), jnp.bfloat16),
        in_specs=[
            pl.BlockSpec((block, features), lambda i: (i, 0)),
            pl.BlockSpec((block, 1), lambda i: (i, 0)),
            pl.BlockSpec((block, 1), lambda i: (i, 0)),
            pl.BlockSpec((width, features), lambda i: (0, 0)),
            pl.BlockSpec((1, width), lambda i: (0, 0)),
            pl.BlockSpec((1, width), lambda i: (0, 0)),
        ],
        out_specs=pl.BlockSpec((block, width), lambda i: (i, 0)),
        compiler_params=pltpu.CompilerParams(vmem_limit_bytes=52 * MIB),
        cost_estimate=pl.CostEstimate(
            flops=8 * count * width * features, bytes_accessed=2 * count * width, transcendentals=count * width
        ),
        name="tile",
    )(points, point_squares[:, None], ids[:, None], chosen, panel_squares[None, :], panel[None, :])


def product_kernel(*refs):
    *tile_refs, here_ref, there_ref, out_ref = refs
    blocks = here_ref.shape[0]
    total = jnp.zeros(out_ref.shape, jnp.float32)
    for part, tile_ref in enumerate(tile_refs):
        update = here_ref[part] if part < blocks else there_ref[part - blocks]
        total = total + lax.dot_general(
            tile_ref[...], update, TRANSPOSED, preferred_element_type=jnp.float32
        )
    out_ref[...] = total


def product(tile, here, there, first, count):
    blocks, targets, width = here.shape
    line = 256
    skip = first // line
    panel = tile.shape[1]
    whole = pl.BlockSpec(here.shape, lambda i: (0, 0, 0))
    parts = [pl.BlockSpec((line, width), lambda i, part=part: (i + skip, part)) for part in range(2 * blocks)]
    return pl.pallas_call(
        product_kernel,
        grid=(count // line,),
        out_shape=jax.ShapeDtypeStruct((count, targets), jnp.float32),
        in_specs=[*parts, whole, whole],
        out_specs=pl.BlockSpec((line, targets), lambda i: (i, 0)),
        compiler_params=pltpu.CompilerParams(vmem_limit_bytes=52 * MIB),
        cost_estimate=pl.CostEstimate(
            flops=4 * count * panel * targets, bytes_accessed=2 * count * panel, transcendentals=0
        ),
        name="product",
    )(*[tile] * len(parts), here, there)


def finish_kernel(half_ref, rest_ref, out_ref):
    blocks, _, width = half_ref.shape
    for block in range(blocks):
        whole = half_ref[block].astype(jnp.float32) + rest_ref[block].astype(jnp.float32)
        out_ref[pl.ds(block * width, width), :] = whole.T


def finish(half, rest):
    blocks, targets, width = half.shape
    vmem = pl.BlockSpec(memory_space=pltpu.VMEM)
    return pl.pallas_call(
        finish_kernel,
        out_shape=jax.ShapeDtypeStruct((blocks * width, targets), jnp.float32),
        in_specs=[vmem] * 2,
        out_specs=vmem,
        compiler_params=pltpu.CompilerParams(vmem_limit_bytes=16 * MIB),
        cost_estimate=pl.CostEstimate(flops=10**6, bytes_accessed=2 * 10**6, transcendentals=0),
        name="finish",
    )(half, rest)


def shift(value, axis, by):
    size = lax.axis_size(axis)
    return lax.ppermute(value, axis, [(i, (i + by) % size) for i in range(size)])


def ring_gather(value, axis):
    half = value.shape[0] // 2
    before = shift(value, axis, 1)
    after = shift(value, axis, -1)
    top = shift(before[:half], axis, 1)
    bottom = shift(after[half:], axis, -1)
    return [value, after, jnp.concatenate([top, bottom], axis=0), before]


def on_device(points, gradient, panel_index):
    own, features = points.shape
    targets = gradient.shape[1]
    blocks, width = panel_index.shape
    shard = blocks * width
    zs, ys, xs, ks = (lax.axis_size(name) for name in DEVICES)
    z, y, x, core = (lax.axis_index(name) for name in DEVICES)
    rows, cols = zs * ys, xs * ks
    row = z * ys + y
    group_start = row * own * cols
    share = shard // rows
    groups = targets // FEW

    tables = [panel_index] + [shift(panel_index, "x", by) for by in range(1, xs)]
    other_points = shift(points, "k", 1)
    other_grads = shift(gradient, "k", 1)
    own_share = lax.dynamic_index_in_dim(panel_index.reshape(rows, share), row, 0, False)
    block = row // groups
    block_index = lax.dynamic_index_in_dim(panel_index, block, 0, False)
    start = (row * xs + x) * own * ks
    rounds, rank = ranks(tables, block_index)
    rounds = jnp.maximum(rounds, shift(rounds, "k", 1))

    def exchange(message):
        return lax.all_to_all(message, ROUTE, 0, 0)

    def exchange_by_axis(message):
        message = message.reshape(xs, zs, ys, SLOTS, 128)
        for dim, axis in enumerate(ROUTE):
            message = lax.all_to_all(message, axis, dim, dim, tiled=True)
        return message

    def route(number, exchange):
        scalars = jnp.stack([number, start, x, core]).astype(jnp.int32)
        message = pack(scalars, tables, points, other_points, gradient, other_grads).reshape(rows * xs, SLOTS, 128)
        message = exchange(message).reshape(rows * xs * SLOTS, 128)
        return place(scalars, message, own_share, block_index, rank, rows)

    def further(state):
        number, piece, right = state
        more_piece, more_right = route(number, exchange_by_axis)
        return number + 1, piece + more_piece, right + more_right

    piece, right_side = route(jnp.int32(0), exchange)
    last = rounds[0, 0]
    _, piece, right_side = lax.while_loop(
        lambda state: state[0] < last, further, (jnp.int32(1), piece, right_side)
    )
    chosen = lax.all_to_all(piece, ROWS, 0, 0).reshape(shard, features)

    own_block = lax.dynamic_index_in_dim(chosen.reshape(blocks, width, features), block, 0, False)
    half, rest = solve(own_block, right_side, rows)
    half = lax.all_to_all(half, ROWS, 0, 0).reshape(blocks, targets, width)

    calm_points, _ = lax.optimization_barrier((points, tables))
    mine, after, far, before = ring_gather(calm_points, "x")
    core_points = jnp.concatenate([far, after, before, mine])
    indices = panel_index.reshape(-1)
    both_chosen = jnp.concatenate([chosen, shift(chosen, "k", 1)])
    both_panel = jnp.concatenate([indices, shift(indices, "k", 1)])
    ahead = (x + jnp.array([2, 1, 3, 0], jnp.int32)) % xs
    ids = group_start + (ahead * ks + core)[:, None] * own + jnp.arange(own, dtype=jnp.int32)[None, :]
    tile = build_tile(core_points, ids.reshape(-1), both_chosen, both_panel)

    half, tile, rest = lax.optimization_barrier((half, tile, rest))
    rest = lax.all_to_all(rest, ROWS, 0, 0).reshape(blocks, targets, width)
    other = shift(half, "k", 1)

    far = product(tile, half, other, 0, own)
    near = product(tile, half, other, own, 2 * own)
    mine = product(tile, half, other, 3 * own, own)
    middle = own // 2
    top = shift(far[:middle], "x", 1)
    bottom = shift(far[middle:], "x", -1)
    send_after = jnp.concatenate([near[:middle] + top, near[middle:own]])
    send_before = jnp.concatenate([near[own : own + middle], near[own + middle :] + bottom])
    from_before = shift(send_after, "x", 1)
    from_after = shift(send_before, "x", -1)
    new_gradient = gradient + (mine + from_before + from_after)
    return new_gradient, finish(half, rest)


def solution(mesh):
    fine = Mesh(mesh.devices.reshape(8, 4, 4, 2), DEVICES)
    in_specs = (P(DEVICES, None), P(DEVICES, None), P(("x", "k"), None))
    out_specs = (P(DEVICES, None), P(("x", "k"), None))
    return jax.shard_map(on_device, mesh=fine, in_specs=in_specs, out_specs=out_specs, check_vma=False)
```

```python
import jax
import jax.numpy as jnp
from jax import lax
from jax.experimental import pallas as pl
from jax.experimental.pallas import tpu as pltpu
from jax.sharding import Mesh
from jax.sharding import PartitionSpec as P

ITERS = 8
RIDGE = 1.0
LOG2E = 1.4426950408889634
DEVICES = ("zh", "zl", "y", "x", "k")
ROUTE = ("x", "zh", "zl", "y")
ROWS = ("zh", "zl", "y")
NEAR = ("zl", "y")
TRANSPOSED = (((1,), (1,)), ((), ()))
FIRST = (((0,), (0,)), ((), ()))
MIB = 1 << 20
POINT_SLOTS = 12
PIECES = 2
GRAD_SLOTS = 32
SLOTS = 16
FEW = 8
CHIPS = 128
XS = 4
OWN = 1024
SHARE = 256
NONE = 1 << 20


def iota(shape, axis):
    return lax.broadcasted_iota(jnp.int32, shape, axis)


def owner_place(index, own, xs, rows):
    chip = index // own
    return (chip % xs) * rows + chip // xs


def pack_kernel(
    scalar_ref, here_ref, one_ref, two_ref, three_ref, points_ref, other_points_ref, grads_ref, other_grads_ref,
    out_ref, values_ref, rows_ref, table_ref,
):
    tables = (here_ref, one_ref, two_ref, three_ref)
    per_shard, width = here_ref.shape
    each, targets = grads_ref.shape
    own = 2 * each
    groups = targets // FEW
    blocks = len(tables) * per_shard
    devices = blocks * groups
    share = width // groups
    per = 128 // FEW
    number = scalar_ref[0]
    for back, table in enumerate(tables):
        shard = (scalar_ref[2] - back) & (len(tables) - 1)
        for lane in range(0, width, 128):
            pair = table[:, lane : lane + 128]
            turned = pltpu.roll(pair, share, 1)
            for block in range(per_shard):
                line = (shard * per_shard + block) * groups + lane // share
                table_ref[pl.ds(line, 1), :] = pair[block : block + 1]
                table_ref[pl.ds(line + 1, 1), :] = turned[block : block + 1]
    offset = table_ref[:, :share] - scalar_ref[1]
    mine = (offset >= 0) & (offset < own)
    held = mine.astype(jnp.bfloat16)
    offset = jnp.where(scalar_ref[3] == 0, offset, jnp.where(offset < each, offset + each, offset - each))
    code = jnp.where(mine, (offset + 1).astype(jnp.float32), 0.0)
    upper = (iota((share, share), 0) < iota((share, share), 1)).astype(jnp.bfloat16)
    rank = jnp.dot(held, upper, preferred_element_type=jnp.float32)
    count = jnp.dot(held, jnp.ones((share, share), jnp.bfloat16), preferred_element_type=jnp.float32)
    left, right = iota((devices, devices), 0), iota((devices, devices), 1)
    earlier = ((left // groups == right // groups) & (right < left)).astype(jnp.bfloat16)
    before = jnp.dot(earlier, count.astype(jnp.bfloat16), preferred_element_type=jnp.float32)
    block_rank = rank + before
    span = SHARE // share
    earlier = ((left // span == right // span) & (right < left)).astype(jnp.bfloat16)
    rank = rank + jnp.dot(earlier, count.astype(jnp.bfloat16), preferred_element_type=jnp.float32)

    lanes = iota((devices, 128), 1)
    first = (number * POINT_SLOTS).astype(jnp.float32)
    found = jnp.zeros((devices, 128), jnp.float32)
    for slot in range(POINT_SLOTS):
        chosen = jnp.sum(jnp.where(rank == first + slot, code, 0.0), axis=1, keepdims=True)
        high = jnp.floor(chosen * 0.125)
        found = jnp.where(lanes == slot, high, jnp.where(lanes == slot + 64, chosen - 8.0 * high, found))
    lines = devices // len(tables)
    shares = lines // span
    reach = ((left // lines == right // lines) & (left % shares == right % lines // span)).astype(jnp.bfloat16)
    found = jnp.dot(reach, found.astype(jnp.bfloat16), preferred_element_type=jnp.float32)
    lanes = iota((devices, own), 1)
    for slot in range(POINT_SLOTS):
        chosen = 8.0 * found[:, slot : slot + 1] + found[:, slot + 64 : slot + 65]
        pick = (lanes + 1 == chosen.astype(jnp.int32)).astype(jnp.bfloat16)
        rows_ref[pl.ds(slot, devices, stride=SLOTS), :] = jnp.dot(
            pick[:, :each], points_ref[...], preferred_element_type=jnp.float32
        ) + jnp.dot(pick[:, each:], other_points_ref[...], preferred_element_type=jnp.float32)

    lanes = iota((devices, 128), 1)
    keep = iota((blocks, 128), 1) // per == iota((blocks, 128), 0)
    parts = []
    left = jnp.concatenate([grads_ref[...], other_grads_ref[...]], axis=0)
    for _ in range(PIECES):
        part = left.astype(jnp.bfloat16)
        left = left - part.astype(jnp.float32)
        parts.append(part)

    @pl.loop(0, GRAD_SLOTS // per)
    def _(turn):
        first = (number * GRAD_SLOTS + turn * per).astype(jnp.float32)
        found = jnp.zeros((devices, 128), jnp.float32)
        for slot in range(per):
            chosen = jnp.sum(jnp.where(block_rank == first + slot, code, 0.0), axis=1, keepdims=True)
            found = jnp.where(lanes % per == slot, chosen, found)
        found = jnp.sum(found.reshape(blocks, groups, 128), axis=1)
        found = jnp.sum(jnp.where(keep, found, 0.0), axis=0, keepdims=True).astype(jnp.int32)
        pick = (iota((own, 128), 0) + 1 == found).astype(jnp.bfloat16)
        values = jnp.zeros((targets, 128), jnp.float32)
        for part in parts:
            values = values + lax.dot_general(part, pick, FIRST, preferred_element_type=jnp.float32)
        values_ref[...] = values
        places = iota((groups, 128), 1) // per
        message = [jnp.zeros((groups, 128), jnp.float32) for _ in range(blocks)]
        for target in range(FEW):
            taken = values_ref[pl.ds(target, groups, stride=FEW), :]
            for block in range(blocks):
                by = (target - block) * per % 128
                turned = pltpu.roll(taken, by, 1) if by else taken
                message[block] = jnp.where(places == target, turned, message[block])
        rest = jnp.concatenate(message, axis=0)
        for place in range(PIECES):
            part = rest.astype(jnp.bfloat16).astype(jnp.float32)
            rest = rest - part
            rows_ref[pl.ds(POINT_SLOTS + PIECES * turn + place, devices, stride=SLOTS), :] = part

    out_ref[...] = rows_ref[...].astype(jnp.bfloat16)


def pack(scalars, tables, points, other_points, grads, other_grads):
    targets = grads.shape[1]
    devices = len(tables) * tables[0].shape[0] * targets // FEW
    vmem = pl.BlockSpec(memory_space=pltpu.VMEM)
    return pl.pallas_call(
        pack_kernel,
        out_shape=jax.ShapeDtypeStruct((devices * SLOTS, 128), jnp.bfloat16),
        in_specs=[pl.BlockSpec(memory_space=pltpu.SMEM)] + [vmem] * 8,
        out_specs=vmem,
        scratch_shapes=[
            pltpu.VMEM((targets, 128), jnp.float32),
            pltpu.VMEM((devices * SLOTS, 128), jnp.float32),
            pltpu.VMEM((devices, 128), jnp.int32),
        ],
        compiler_params=pltpu.CompilerParams(vmem_limit_bytes=16 * MIB),
        name="pack",
    )(scalars, *tables, points, other_points, grads, other_grads)


def ranks_kernel(here_ref, one_ref, two_ref, three_ref, block_row_ref, block_column_ref, rounds_ref, rank_ref):
    tables = (here_ref, one_ref, two_ref, three_ref)
    per_shard, width = here_ref.shape
    share = SHARE
    segments = iota((width, 128), 0) // share == iota((width, 128), 1)
    segments = segments | (iota((width, 128), 1) == 127)
    segments = segments.astype(jnp.bfloat16)
    most = jnp.zeros((CHIPS, 128), jnp.float32)
    chip = iota((CHIPS, width), 0)

    def count(block, most):
        for table in tables:
            hit = (chip == table[pl.ds(block, 1), :] // OWN).astype(jnp.bfloat16)
            most = jnp.maximum(most, jnp.dot(hit, segments, preferred_element_type=jnp.float32))
        return most

    most = lax.fori_loop(0, per_shard, count, most)
    whole = iota((CHIPS, 128), 1) == 127
    most_block = jnp.max(jnp.where(whole, most, 0.0), keepdims=True).astype(jnp.int32)
    most_share = jnp.max(jnp.where(whole, 0.0, most), keepdims=True).astype(jnp.int32)
    rounds_ref[...] = jnp.maximum(
        (most_block + GRAD_SLOTS - 1) // GRAD_SLOTS, (most_share + POINT_SLOTS - 1) // POINT_SLOTS
    )
    owners = block_row_ref[...] // OWN
    step = 128

    def compare(number, total):
        start = pl.multiple_of(number * step, step)
        others = block_column_ref[pl.ds(start, step), :] // OWN
        earlier = iota((step, width), 0) + start < iota((step, width), 1)
        same = jnp.where((others == owners) & earlier, 1, 0)
        return total + jnp.sum(same.reshape(step // 8, 8, width), axis=0)

    total = lax.fori_loop(0, width // step, compare, jnp.zeros((8, width), jnp.int32))
    rank_ref[...] = jnp.sum(total, axis=0, keepdims=True)


def ranks(tables, block_index):
    vmem = pl.BlockSpec(memory_space=pltpu.VMEM)
    width = block_index.shape[0]
    return pl.pallas_call(
        ranks_kernel,
        out_shape=(
            jax.ShapeDtypeStruct((1, 1), jnp.int32),
            jax.ShapeDtypeStruct((1, width), jnp.int32),
        ),
        in_specs=[vmem] * 6,
        out_specs=(vmem, vmem),
        compiler_params=pltpu.CompilerParams(vmem_limit_bytes=16 * MIB),
        cost_estimate=pl.CostEstimate(flops=4 * 10**9, bytes_accessed=10**5, transcendentals=0),
        name="ranks",
    )(*tables, block_index[None, :], block_index[:, None])


def place_kernel(scalar_ref, message_ref, row_ref, column_ref, block_ref, rank_ref, piece_ref, right_ref):
    length = message_ref.shape[0]
    share = column_ref.shape[0]
    width = block_ref.shape[1]
    per = 128 // FEW
    turns = GRAD_SLOTS // per
    number = scalar_ref[0]
    row_owner = owner_place(row_ref[...], OWN, XS, CHIPS // XS)
    column_owner = owner_place(column_ref[...], OWN, XS, CHIPS // XS)
    earlier = iota((share, share), 1) < iota((share, share), 0)
    rank = jnp.sum(
        jnp.where((row_owner == column_owner) & earlier, 1.0, 0.0), axis=1, keepdims=True
    ).astype(jnp.int32)
    slot = rank - number * POINT_SLOTS
    code = jnp.where((slot >= 0) & (slot < POINT_SLOTS), column_owner * SLOTS + slot, -1)
    slot = rank_ref[...] - number * GRAD_SLOTS
    wanted = owner_place(block_ref[...], OWN, XS, CHIPS // XS) * turns + slot // per
    wanted = jnp.where((slot >= 0) & (slot < GRAD_SLOTS), wanted, -NONE)
    step = 256
    def gather(number, state):
        found, piece = state
        start = pl.multiple_of(number * step, step)
        message = message_ref[pl.ds(start, step), :]
        line = iota((step, width), 0)
        turn = (line % SLOTS - POINT_SLOTS + PIECES) // PIECES - 1
        source = jnp.where((turn >= 0) & (turn < turns), line // SLOTS * turns + turn, 2 * NONE)
        pick = (source == wanted - number * (step // SLOTS * turns)).astype(jnp.bfloat16)
        found = found + lax.dot_general(message, pick, FIRST, preferred_element_type=jnp.float32)
        pick = (iota((share, step), 1) == code - start).astype(jnp.bfloat16)
        return found, piece + jnp.dot(pick, message, preferred_element_type=jnp.float32)

    state = jnp.zeros((128, width), jnp.float32), jnp.zeros((share, 128), jnp.float32)
    found, piece = lax.fori_loop(0, length // step, gather, state)
    piece = piece.astype(jnp.bfloat16)
    for copy in range(piece_ref.shape[0]):
        piece_ref[copy] = piece
    here = iota((per, width), 0) == slot % per
    for target in range(FEW):
        part = found[target * per : (target + 1) * per]
        right_ref[pl.ds(target, 1), :] = -jnp.sum(jnp.where(here, part, 0.0), axis=0, keepdims=True)


def place(scalars, message, index, block_index, rank, copies):
    vmem = pl.BlockSpec(memory_space=pltpu.VMEM)
    share, width = index.shape[0], block_index.shape[0]
    return pl.pallas_call(
        place_kernel,
        out_shape=(
            jax.ShapeDtypeStruct((copies, share, 128), jnp.bfloat16),
            jax.ShapeDtypeStruct((FEW, width), jnp.float32),
        ),
        in_specs=[pl.BlockSpec(memory_space=pltpu.SMEM)] + [vmem] * 5,
        out_specs=(vmem, vmem),
        compiler_params=pltpu.CompilerParams(vmem_limit_bytes=16 * MIB),
        name="place",
    )(scalars, message, index[None, :], index[:, None], block_index[None, :], rank)


def solve_kernel(points_ref, right_ref, half_ref, rest_ref, high_ref, low_ref):
    width = points_ref.shape[0]
    scale = -2.0 / points_ref.shape[1] * LOG2E
    step = 256
    same = iota((step, step), 0) == iota((step, step), 1)
    columns, lines = [], []
    for start in range(0, width, step):
        part = points_ref[pl.ds(start, step), :]
        inner = lax.dot_general(part, part, TRANSPOSED, preferred_element_type=jnp.float32)
        inner = jnp.where(same, inner, 0.0)
        columns.append(jnp.sum(inner, axis=1, keepdims=True))
        lines.append(jnp.sum(inner, axis=0, keepdims=True))
    line = jnp.concatenate(lines, axis=1)
    upper = jnp.zeros((1, 1), jnp.float32)
    for number, start in enumerate(range(0, width, step)):
        piece = pl.ds(start, step)
        inner = lax.dot_general(
            points_ref[piece, :], points_ref[...], TRANSPOSED, preferred_element_type=jnp.float32
        )
        distance = jnp.maximum(columns[number] + line - 2.0 * inner, 0.0)
        values = jnp.exp2(distance * scale)
        sums = jnp.sum(values, axis=1, keepdims=True)
        upper = jnp.maximum(upper, jnp.max(sums, axis=0, keepdims=True))
        high = values.astype(jnp.bfloat16)
        high_ref[piece, :] = high
        low_ref[piece, :] = (values - high.astype(jnp.float32)).astype(jnp.bfloat16)
    upper = upper + RIDGE
    center = (upper + RIDGE) / 2.0
    radius = (upper - RIDGE) / 2.0
    ratio = center / radius
    factor = 1.0 / ratio
    residual = right_ref[...]
    targets = residual.shape[0]
    direction = residual / center
    update = jnp.zeros_like(residual)
    for iteration in range(ITERS):
        update = update + direction
        if iteration < ITERS - 1:
            high = direction.astype(jnp.bfloat16)
            low = (direction - high.astype(jnp.float32)).astype(jnp.bfloat16)
            both = jnp.concatenate([high, low], axis=0)
            main = jnp.dot(both, high_ref[...], preferred_element_type=jnp.float32)
            rest = jnp.dot(high, low_ref[...], preferred_element_type=jnp.float32)
            product = main[:targets] + (main[targets:] + rest)
            residual = residual - (product + RIDGE * direction)
            following = 1.0 / (2.0 * ratio - factor)
            direction = following * factor * direction + 2.0 * following / radius * residual
            factor = following
    half = update.astype(jnp.bfloat16)
    rest = (update - half.astype(jnp.float32)).astype(jnp.bfloat16)
    for copy in range(half_ref.shape[0]):
        half_ref[copy] = half
        rest_ref[copy] = rest


def solve(points, right_side, copies):
    width, _ = points.shape
    vmem = pl.BlockSpec(memory_space=pltpu.VMEM)
    return pl.pallas_call(
        solve_kernel,
        out_shape=(jax.ShapeDtypeStruct((copies, *right_side.shape), jnp.bfloat16),) * 2,
        in_specs=[vmem] * 2,
        out_specs=(vmem, vmem),
        scratch_shapes=[pltpu.VMEM((width, width), jnp.bfloat16)] * 2,
        compiler_params=pltpu.CompilerParams(vmem_limit_bytes=16 * MIB),
        cost_estimate=pl.CostEstimate(flops=6 * 10**9, bytes_accessed=10**6, transcendentals=width * width),
        name="solve",
    )(points, right_side)


def tile_kernel(points_ref, column_ref, ids_ref, chosen_ref, row_ref, panel_ref, out_ref):
    scale = -2.0 / points_ref.shape[1] * LOG2E
    step = 512
    for start in range(0, chosen_ref.shape[0], step):
        piece = pl.ds(start, step)
        inner = lax.dot_general(
            points_ref[...], chosen_ref[piece, :], TRANSPOSED, preferred_element_type=jnp.float32
        )
        distance = jnp.maximum(column_ref[...] + row_ref[:, piece] - 2.0 * inner, 0.0)
        values = jnp.exp2(distance * scale)
        values = jnp.where(ids_ref[...] == panel_ref[:, piece], values + RIDGE, values)
        out_ref[:, piece] = values.astype(jnp.bfloat16)


def build_tile(points, ids, chosen, panel):
    count, features = points.shape
    width = chosen.shape[0]
    block = 256
    point_squares = jnp.sum(jnp.square(points.astype(jnp.float32)), axis=-1)
    panel_squares = jnp.sum(jnp.square(chosen.astype(jnp.float32)), axis=-1)
    return pl.pallas_call(
        tile_kernel,
        grid=(count // block,),
        out_shape=jax.ShapeDtypeStruct((count, width), jnp.bfloat16),
        in_specs=[
            pl.BlockSpec((block, features), lambda i: (i, 0)),
            pl.BlockSpec((block, 1), lambda i: (i, 0)),
            pl.BlockSpec((block, 1), lambda i: (i, 0)),
            pl.BlockSpec((width, features), lambda i: (0, 0)),
            pl.BlockSpec((1, width), lambda i: (0, 0)),
            pl.BlockSpec((1, width), lambda i: (0, 0)),
        ],
        out_specs=pl.BlockSpec((block, width), lambda i: (i, 0)),
        compiler_params=pltpu.CompilerParams(vmem_limit_bytes=52 * MIB),
        cost_estimate=pl.CostEstimate(
            flops=8 * count * width * features, bytes_accessed=2 * count * width, transcendentals=count * width
        ),
        name="tile",
    )(points, point_squares[:, None], ids[:, None], chosen, panel_squares[None, :], panel[None, :])


def product_kernel(*refs):
    *tile_refs, here_ref, there_ref, out_ref = refs
    blocks = here_ref.shape[0]
    total = jnp.zeros(out_ref.shape, jnp.float32)
    for part, tile_ref in enumerate(tile_refs):
        update = here_ref[part] if part < blocks else there_ref[part - blocks]
        total = total + lax.dot_general(
            tile_ref[...], update, TRANSPOSED, preferred_element_type=jnp.float32
        )
    out_ref[...] = total


def product(tile, here, there, first, count):
    blocks, targets, width = here.shape
    line = 256
    skip = first // line
    panel = tile.shape[1]
    whole = pl.BlockSpec(here.shape, lambda i: (0, 0, 0))
    parts = [pl.BlockSpec((line, width), lambda i, part=part: (i + skip, part)) for part in range(2 * blocks)]
    return pl.pallas_call(
        product_kernel,
        grid=(count // line,),
        out_shape=jax.ShapeDtypeStruct((count, targets), jnp.float32),
        in_specs=[*parts, whole, whole],
        out_specs=pl.BlockSpec((line, targets), lambda i: (i, 0)),
        compiler_params=pltpu.CompilerParams(vmem_limit_bytes=52 * MIB),
        cost_estimate=pl.CostEstimate(
            flops=4 * count * panel * targets, bytes_accessed=2 * count * panel, transcendentals=0
        ),
        name="product",
    )(*[tile] * len(parts), here, there)


def finish_kernel(half_ref, rest_ref, out_ref):
    blocks, _, width = half_ref.shape
    for block in range(blocks):
        whole = half_ref[block].astype(jnp.float32) + rest_ref[block].astype(jnp.float32)
        out_ref[pl.ds(block * width, width), :] = whole.T


def finish(half, rest):
    blocks, targets, width = half.shape
    vmem = pl.BlockSpec(memory_space=pltpu.VMEM)
    return pl.pallas_call(
        finish_kernel,
        out_shape=jax.ShapeDtypeStruct((blocks * width, targets), jnp.float32),
        in_specs=[vmem] * 2,
        out_specs=vmem,
        compiler_params=pltpu.CompilerParams(vmem_limit_bytes=16 * MIB),
        cost_estimate=pl.CostEstimate(flops=10**6, bytes_accessed=2 * 10**6, transcendentals=0),
        name="finish",
    )(half, rest)


def shift(value, axis, by):
    size = lax.axis_size(axis)
    return lax.ppermute(value, axis, [(i, (i + by) % size) for i in range(size)])


def ring_gather(value, axis):
    half = value.shape[0] // 2
    before = shift(value, axis, 1)
    after = shift(value, axis, -1)
    top = shift(before[:half], axis, 1)
    bottom = shift(after[half:], axis, -1)
    return [value, after, jnp.concatenate([top, bottom], axis=0), before]


def on_device(points, gradient, panel_index):
    own, features = points.shape
    targets = gradient.shape[1]
    blocks, width = panel_index.shape
    shard = blocks * width
    rows, near, xs, ks = (lax.axis_size(name) for name in (ROWS, NEAR, "x", "k"))
    cols = xs * ks
    row, x, core = lax.axis_index(ROWS), lax.axis_index("x"), lax.axis_index("k")
    group_start = row * own * cols
    share = shard // near
    groups = targets // FEW

    tables = [panel_index] + [shift(panel_index, "x", by) for by in range(1, xs)]
    other_points = shift(points, "k", 1)
    other_grads = shift(gradient, "k", 1)
    own_share = lax.dynamic_index_in_dim(panel_index.reshape(near, share), row % near, 0, False)
    block = row // groups
    block_index = lax.dynamic_index_in_dim(panel_index, block, 0, False)
    start = (row * xs + x) * own * ks
    rounds, rank = ranks(tables, block_index)
    rounds = jnp.maximum(rounds, shift(rounds, "k", 1))

    def exchange(message):
        return lax.all_to_all(message, ROUTE, 0, 0)

    def exchange_by_axis(message):
        message = message.reshape(*(lax.axis_size(axis) for axis in ROUTE), SLOTS, 128)
        for dim, axis in enumerate(ROUTE):
            message = lax.all_to_all(message, axis, dim, dim, tiled=True)
        return message

    def route(number, exchange):
        scalars = jnp.stack([number, start, x, core]).astype(jnp.int32)
        message = pack(scalars, tables, points, other_points, gradient, other_grads).reshape(rows * xs, SLOTS, 128)
        message = exchange(message).reshape(rows * xs * SLOTS, 128)
        return place(scalars, message, own_share, block_index, rank, near)

    def further(state):
        number, piece, right = state
        more_piece, more_right = route(number, exchange_by_axis)
        return number + 1, piece + more_piece, right + more_right

    piece, right_side = route(jnp.int32(0), exchange)
    last = rounds[0, 0]
    _, piece, right_side = lax.while_loop(
        lambda state: state[0] < last, further, (jnp.int32(1), piece, right_side)
    )
    chosen = lax.all_to_all(piece, NEAR, 0, 0).reshape(shard, features)

    own_block = lax.dynamic_index_in_dim(chosen.reshape(blocks, width, features), block, 0, False)
    half, rest = solve(own_block, right_side, rows)
    half = lax.all_to_all(half, ROWS, 0, 0).reshape(blocks, targets, width)

    calm_points, _ = lax.optimization_barrier((points, tables))
    mine, after, far, before = ring_gather(calm_points, "x")
    core_points = jnp.concatenate([far, after, before, mine])
    indices = panel_index.reshape(-1)
    both_chosen = jnp.concatenate([chosen, shift(chosen, "k", 1)])
    both_panel = jnp.concatenate([indices, shift(indices, "k", 1)])
    ahead = (x + jnp.array([2, 1, 3, 0], jnp.int32)) % xs
    ids = group_start + (ahead * ks + core)[:, None] * own + jnp.arange(own, dtype=jnp.int32)[None, :]
    tile = build_tile(core_points, ids.reshape(-1), both_chosen, both_panel)

    half, tile, rest = lax.optimization_barrier((half, tile, rest))
    rest = lax.all_to_all(rest, ROWS, 0, 0).reshape(blocks, targets, width)
    other = shift(half, "k", 1)

    far = product(tile, half, other, 0, own)
    near = product(tile, half, other, own, 2 * own)
    mine = product(tile, half, other, 3 * own, own)
    middle = own // 2
    top = shift(far[:middle], "x", 1)
    bottom = shift(far[middle:], "x", -1)
    send_after = jnp.concatenate([near[:middle] + top, near[middle:own]])
    send_before = jnp.concatenate([near[own : own + middle], near[own + middle :] + bottom])
    from_before = shift(send_after, "x", 1)
    from_after = shift(send_before, "x", -1)
    new_gradient = gradient + (mine + from_before + from_after)
    return new_gradient, finish(half, rest)


def solution(mesh):
    fine = Mesh(mesh.devices.reshape(4, 2, 4, 4, 2), DEVICES)
    in_specs = (P(DEVICES, None), P(DEVICES, None), P(("x", "k"), None))
    out_specs = (P(DEVICES, None), P(("x", "k"), None))
    return jax.shard_map(on_device, mesh=fine, in_specs=in_specs, out_specs=out_specs, check_vma=False)
```

```python
import functools

import jax
import jax.numpy as jnp
from jax import lax
from jax.experimental import pallas as pl
from jax.experimental.pallas import tpu as pltpu
from jax.sharding import Mesh
from jax.sharding import PartitionSpec as P

ITERS = 8
RIDGE = 1.0
LOG2E = 1.4426950408889634
DEVICES = ("zh", "zl", "y", "x", "k")
ROUTE = ("x", "zh", "zl", "y")
ROWS = ("zh", "zl", "y")
NEAR = ("zl", "y")
TRANSPOSED = (((1,), (1,)), ((), ()))
FIRST = (((0,), (0,)), ((), ()))
MIB = 1 << 20
POINT_SLOTS = 12
PIECES = 2
GRAD_SLOTS = 32
SLOTS = 16
FEW = 8
CHIPS = 128
XS = 4
OWN = 1024
SHARE = 256
NONE = 1 << 20


def iota(shape, axis):
    return lax.broadcasted_iota(jnp.int32, shape, axis)


def owner_place(index, own, xs, rows):
    chip = index // own
    return (chip % xs) * rows + chip // xs


def pack_kernel(
    scalar_ref, here_ref, one_ref, two_ref, three_ref, points_ref, other_points_ref, grads_ref, other_grads_ref,
    out_ref, values_ref, rows_ref, table_ref, *, unroll,
):
    tables = (here_ref, one_ref, two_ref, three_ref)
    per_shard, width = here_ref.shape
    each, targets = grads_ref.shape
    own = 2 * each
    groups = targets // FEW
    blocks = len(tables) * per_shard
    devices = blocks * groups
    share = width // groups
    per = 128 // FEW
    number = scalar_ref[0]
    for back, table in enumerate(tables):
        shard = (scalar_ref[2] - back) & (len(tables) - 1)
        for lane in range(0, width, 128):
            pair = table[:, lane : lane + 128]
            turned = pltpu.roll(pair, share, 1)
            for block in range(per_shard):
                line = (shard * per_shard + block) * groups + lane // share
                table_ref[pl.ds(line, 1), :] = pair[block : block + 1]
                table_ref[pl.ds(line + 1, 1), :] = turned[block : block + 1]
    offset = table_ref[:, :share] - scalar_ref[1]
    mine = (offset >= 0) & (offset < own)
    held = mine.astype(jnp.bfloat16)
    offset = jnp.where(scalar_ref[3] == 0, offset, jnp.where(offset < each, offset + each, offset - each))
    code = jnp.where(mine, (offset + 1).astype(jnp.float32), 0.0)
    upper = (iota((share, share), 0) < iota((share, share), 1)).astype(jnp.bfloat16)
    rank = jnp.dot(held, upper, preferred_element_type=jnp.float32)
    count = jnp.dot(held, jnp.ones((share, share), jnp.bfloat16), preferred_element_type=jnp.float32)
    left, right = iota((devices, devices), 0), iota((devices, devices), 1)
    earlier = ((left // groups == right // groups) & (right < left)).astype(jnp.bfloat16)
    before = jnp.dot(earlier, count.astype(jnp.bfloat16), preferred_element_type=jnp.float32)
    block_rank = rank + before
    span = SHARE // share
    earlier = ((left // span == right // span) & (right < left)).astype(jnp.bfloat16)
    rank = rank + jnp.dot(earlier, count.astype(jnp.bfloat16), preferred_element_type=jnp.float32)

    lanes = iota((devices, 128), 1)
    first = (number * POINT_SLOTS).astype(jnp.float32)
    found = jnp.zeros((devices, 128), jnp.float32)
    for slot in range(POINT_SLOTS):
        chosen = jnp.sum(jnp.where(rank == first + slot, code, 0.0), axis=1, keepdims=True)
        high = jnp.floor(chosen * 0.125)
        found = jnp.where(lanes == slot, high, jnp.where(lanes == slot + 64, chosen - 8.0 * high, found))
    lines = devices // len(tables)
    shares = lines // span
    reach = ((left // lines == right // lines) & (left % shares == right % lines // span)).astype(jnp.bfloat16)
    found = jnp.dot(reach, found.astype(jnp.bfloat16), preferred_element_type=jnp.float32)
    lanes = iota((devices, own), 1)
    for slot in range(POINT_SLOTS):
        chosen = 8.0 * found[:, slot : slot + 1] + found[:, slot + 64 : slot + 65]
        pick = (lanes + 1 == chosen.astype(jnp.int32)).astype(jnp.bfloat16)
        rows_ref[pl.ds(slot, devices, stride=SLOTS), :] = jnp.dot(
            pick[:, :each], points_ref[...], preferred_element_type=jnp.float32
        ) + jnp.dot(pick[:, each:], other_points_ref[...], preferred_element_type=jnp.float32)

    lanes = iota((devices, 128), 1)
    keep = iota((blocks, 128), 1) // per == iota((blocks, 128), 0)
    parts = []
    left = jnp.concatenate([grads_ref[...], other_grads_ref[...]], axis=0)
    for _ in range(PIECES):
        part = left.astype(jnp.bfloat16)
        left = left - part.astype(jnp.float32)
        parts.append(part)

    @pl.loop(0, GRAD_SLOTS // per, unroll=unroll)
    def _(turn):
        first = (number * GRAD_SLOTS + turn * per).astype(jnp.float32)
        found = jnp.zeros((devices, 128), jnp.float32)
        for slot in range(per):
            chosen = jnp.sum(jnp.where(block_rank == first + slot, code, 0.0), axis=1, keepdims=True)
            found = jnp.where(lanes % per == slot, chosen, found)
        found = jnp.sum(found.reshape(blocks, groups, 128), axis=1)
        found = jnp.sum(jnp.where(keep, found, 0.0), axis=0, keepdims=True).astype(jnp.int32)
        pick = (iota((own, 128), 0) + 1 == found).astype(jnp.bfloat16)
        values = jnp.zeros((targets, 128), jnp.float32)
        for part in parts:
            values = values + lax.dot_general(part, pick, FIRST, preferred_element_type=jnp.float32)
        values_ref[...] = values
        places = iota((groups, 128), 1) // per
        message = [jnp.zeros((groups, 128), jnp.float32) for _ in range(blocks)]
        for target in range(FEW):
            taken = values_ref[pl.ds(target, groups, stride=FEW), :]
            for block in range(blocks):
                by = (target - block) * per % 128
                turned = pltpu.roll(taken, by, 1) if by else taken
                message[block] = jnp.where(places == target, turned, message[block])
        rest = jnp.concatenate(message, axis=0)
        for place in range(PIECES):
            part = rest.astype(jnp.bfloat16).astype(jnp.float32)
            rest = rest - part
            rows_ref[pl.ds(POINT_SLOTS + PIECES * turn + place, devices, stride=SLOTS), :] = part

    out_ref[...] = rows_ref[...].astype(jnp.bfloat16)


def pack(scalars, tables, points, other_points, grads, other_grads, unroll):
    targets = grads.shape[1]
    devices = len(tables) * tables[0].shape[0] * targets // FEW
    vmem = pl.BlockSpec(memory_space=pltpu.VMEM)
    return pl.pallas_call(
        functools.partial(pack_kernel, unroll=unroll),
        out_shape=jax.ShapeDtypeStruct((devices * SLOTS, 128), jnp.bfloat16),
        in_specs=[pl.BlockSpec(memory_space=pltpu.SMEM)] + [vmem] * 8,
        out_specs=vmem,
        scratch_shapes=[
            pltpu.VMEM((targets, 128), jnp.float32),
            pltpu.VMEM((devices * SLOTS, 128), jnp.float32),
            pltpu.VMEM((devices, 128), jnp.int32),
        ],
        compiler_params=pltpu.CompilerParams(vmem_limit_bytes=16 * MIB),
        name="pack",
    )(scalars, *tables, points, other_points, grads, other_grads)


def ranks_kernel(here_ref, one_ref, two_ref, three_ref, block_row_ref, block_column_ref, rounds_ref, rank_ref):
    tables = (here_ref, one_ref, two_ref, three_ref)
    per_shard, width = here_ref.shape
    share = SHARE
    segments = iota((width, 128), 0) // share == iota((width, 128), 1)
    segments = segments | (iota((width, 128), 1) == 127)
    segments = segments.astype(jnp.bfloat16)
    most = jnp.zeros((CHIPS, 128), jnp.float32)
    chip = iota((CHIPS, width), 0)

    def count(block, most):
        for table in tables:
            hit = (chip == table[pl.ds(block, 1), :] // OWN).astype(jnp.bfloat16)
            most = jnp.maximum(most, jnp.dot(hit, segments, preferred_element_type=jnp.float32))
        return most

    most = lax.fori_loop(0, per_shard, count, most)
    whole = iota((CHIPS, 128), 1) == 127
    most_block = jnp.max(jnp.where(whole, most, 0.0), keepdims=True).astype(jnp.int32)
    most_share = jnp.max(jnp.where(whole, 0.0, most), keepdims=True).astype(jnp.int32)
    rounds_ref[...] = jnp.maximum(
        (most_block + GRAD_SLOTS - 1) // GRAD_SLOTS, (most_share + POINT_SLOTS - 1) // POINT_SLOTS
    )
    owners = block_row_ref[...] // OWN
    step = 128

    def compare(number, total):
        start = pl.multiple_of(number * step, step)
        others = block_column_ref[pl.ds(start, step), :] // OWN
        earlier = iota((step, width), 0) + start < iota((step, width), 1)
        same = jnp.where((others == owners) & earlier, 1, 0)
        return total + jnp.sum(same.reshape(step // 8, 8, width), axis=0)

    total = lax.fori_loop(0, width // step, compare, jnp.zeros((8, width), jnp.int32))
    rank_ref[...] = jnp.sum(total, axis=0, keepdims=True)


def ranks(tables, block_index):
    vmem = pl.BlockSpec(memory_space=pltpu.VMEM)
    width = block_index.shape[0]
    return pl.pallas_call(
        ranks_kernel,
        out_shape=(
            jax.ShapeDtypeStruct((1, 1), jnp.int32),
            jax.ShapeDtypeStruct((1, width), jnp.int32),
        ),
        in_specs=[vmem] * 6,
        out_specs=(vmem, vmem),
        compiler_params=pltpu.CompilerParams(vmem_limit_bytes=16 * MIB),
        cost_estimate=pl.CostEstimate(flops=4 * 10**9, bytes_accessed=10**5, transcendentals=0),
        name="ranks",
    )(*tables, block_index[None, :], block_index[:, None])


def place_kernel(scalar_ref, message_ref, row_ref, column_ref, block_ref, rank_ref, piece_ref, right_ref, *, unroll):
    length = message_ref.shape[0]
    share = column_ref.shape[0]
    width = block_ref.shape[1]
    per = 128 // FEW
    turns = GRAD_SLOTS // per
    number = scalar_ref[0]
    row_owner = owner_place(row_ref[...], OWN, XS, CHIPS // XS)
    column_owner = owner_place(column_ref[...], OWN, XS, CHIPS // XS)
    earlier = iota((share, share), 1) < iota((share, share), 0)
    rank = jnp.sum(
        jnp.where((row_owner == column_owner) & earlier, 1.0, 0.0), axis=1, keepdims=True
    ).astype(jnp.int32)
    slot = rank - number * POINT_SLOTS
    code = jnp.where((slot >= 0) & (slot < POINT_SLOTS), column_owner * SLOTS + slot, -1)
    slot = rank_ref[...] - number * GRAD_SLOTS
    wanted = owner_place(block_ref[...], OWN, XS, CHIPS // XS) * turns + slot // per
    wanted = jnp.where((slot >= 0) & (slot < GRAD_SLOTS), wanted, -NONE)
    step = 256
    def gather(number, state):
        found, piece = state
        start = pl.multiple_of(number * step, step)
        message = message_ref[pl.ds(start, step), :]
        line = iota((step, width), 0)
        turn = (line % SLOTS - POINT_SLOTS + PIECES) // PIECES - 1
        source = jnp.where((turn >= 0) & (turn < turns), line // SLOTS * turns + turn, 2 * NONE)
        pick = (source == wanted - number * (step // SLOTS * turns)).astype(jnp.bfloat16)
        found = found + lax.dot_general(message, pick, FIRST, preferred_element_type=jnp.float32)
        pick = (iota((share, step), 1) == code - start).astype(jnp.bfloat16)
        return found, piece + jnp.dot(pick, message, preferred_element_type=jnp.float32)

    state = jnp.zeros((128, width), jnp.float32), jnp.zeros((share, 128), jnp.float32)
    found, piece = lax.fori_loop(0, length // step, gather, state, unroll=unroll)
    piece = piece.astype(jnp.bfloat16)
    for copy in range(piece_ref.shape[0]):
        piece_ref[copy] = piece
    here = iota((per, width), 0) == slot % per
    for target in range(FEW):
        part = found[target * per : (target + 1) * per]
        right_ref[pl.ds(target, 1), :] = -jnp.sum(jnp.where(here, part, 0.0), axis=0, keepdims=True)


def place(scalars, message, index, block_index, rank, copies, unroll):
    vmem = pl.BlockSpec(memory_space=pltpu.VMEM)
    share, width = index.shape[0], block_index.shape[0]
    return pl.pallas_call(
        functools.partial(place_kernel, unroll=unroll),
        out_shape=(
            jax.ShapeDtypeStruct((copies, share, 128), jnp.bfloat16),
            jax.ShapeDtypeStruct((FEW, width), jnp.float32),
        ),
        in_specs=[pl.BlockSpec(memory_space=pltpu.SMEM)] + [vmem] * 5,
        out_specs=(vmem, vmem),
        compiler_params=pltpu.CompilerParams(vmem_limit_bytes=16 * MIB),
        name="place",
    )(scalars, message, index[None, :], index[:, None], block_index[None, :], rank)


def solve_kernel(points_ref, right_ref, half_ref, rest_ref, high_ref, low_ref):
    width = points_ref.shape[0]
    scale = -2.0 / points_ref.shape[1] * LOG2E
    step = 256
    same = iota((step, step), 0) == iota((step, step), 1)
    columns, lines = [], []
    for start in range(0, width, step):
        part = points_ref[pl.ds(start, step), :]
        inner = lax.dot_general(part, part, TRANSPOSED, preferred_element_type=jnp.float32)
        inner = jnp.where(same, inner, 0.0)
        columns.append(jnp.sum(inner, axis=1, keepdims=True))
        lines.append(jnp.sum(inner, axis=0, keepdims=True))
    line = jnp.concatenate(lines, axis=1)
    upper = jnp.zeros((1, 1), jnp.float32)
    for number, start in enumerate(range(0, width, step)):
        piece = pl.ds(start, step)
        inner = lax.dot_general(
            points_ref[piece, :], points_ref[...], TRANSPOSED, preferred_element_type=jnp.float32
        )
        distance = jnp.maximum(columns[number] + line - 2.0 * inner, 0.0)
        values = jnp.exp2(distance * scale)
        sums = jnp.sum(values, axis=1, keepdims=True)
        upper = jnp.maximum(upper, jnp.max(sums, axis=0, keepdims=True))
        high = values.astype(jnp.bfloat16)
        high_ref[piece, :] = high
        low_ref[piece, :] = (values - high.astype(jnp.float32)).astype(jnp.bfloat16)
    upper = upper + RIDGE
    center = (upper + RIDGE) / 2.0
    radius = (upper - RIDGE) / 2.0
    ratio = center / radius
    factor = 1.0 / ratio
    residual = right_ref[...]
    targets = residual.shape[0]
    direction = residual / center
    update = jnp.zeros_like(residual)
    for iteration in range(ITERS):
        update = update + direction
        if iteration < ITERS - 1:
            high = direction.astype(jnp.bfloat16)
            low = (direction - high.astype(jnp.float32)).astype(jnp.bfloat16)
            both = jnp.concatenate([high, low], axis=0)
            main = jnp.dot(both, high_ref[...], preferred_element_type=jnp.float32)
            rest = jnp.dot(high, low_ref[...], preferred_element_type=jnp.float32)
            product = main[:targets] + (main[targets:] + rest)
            residual = residual - (product + RIDGE * direction)
            following = 1.0 / (2.0 * ratio - factor)
            direction = following * factor * direction + 2.0 * following / radius * residual
            factor = following
    half = update.astype(jnp.bfloat16)
    rest = (update - half.astype(jnp.float32)).astype(jnp.bfloat16)
    for copy in range(half_ref.shape[0]):
        half_ref[copy] = half
        rest_ref[copy] = rest


def solve(points, right_side, copies):
    width, _ = points.shape
    vmem = pl.BlockSpec(memory_space=pltpu.VMEM)
    return pl.pallas_call(
        solve_kernel,
        out_shape=(jax.ShapeDtypeStruct((copies, *right_side.shape), jnp.bfloat16),) * 2,
        in_specs=[vmem] * 2,
        out_specs=(vmem, vmem),
        scratch_shapes=[pltpu.VMEM((width, width), jnp.bfloat16)] * 2,
        compiler_params=pltpu.CompilerParams(vmem_limit_bytes=16 * MIB),
        cost_estimate=pl.CostEstimate(flops=6 * 10**9, bytes_accessed=10**6, transcendentals=width * width),
        name="solve",
    )(points, right_side)


def tile_kernel(points_ref, column_ref, ids_ref, chosen_ref, row_ref, panel_ref, out_ref):
    scale = -2.0 / points_ref.shape[1] * LOG2E
    step = 512

    def part(number, _):
        piece = pl.ds(pl.multiple_of(number * step, step), step)
        inner = lax.dot_general(
            points_ref[...], chosen_ref[piece, :], TRANSPOSED, preferred_element_type=jnp.float32
        )
        distance = jnp.maximum(column_ref[...] + row_ref[:, piece] - 2.0 * inner, 0.0)
        values = jnp.exp2(distance * scale)
        values = jnp.where(ids_ref[...] == panel_ref[:, piece], values + RIDGE, values)
        out_ref[:, piece] = values.astype(jnp.bfloat16)
        return 0

    lax.fori_loop(0, chosen_ref.shape[0] // step, part, 0, unroll=4)


def build_tile(points, ids, chosen, panel):
    count, features = points.shape
    width = chosen.shape[0]
    block = 256
    point_squares = jnp.sum(jnp.square(points.astype(jnp.float32)), axis=-1)
    panel_squares = jnp.sum(jnp.square(chosen.astype(jnp.float32)), axis=-1)
    return pl.pallas_call(
        tile_kernel,
        grid=(count // block,),
        out_shape=jax.ShapeDtypeStruct((count, width), jnp.bfloat16),
        in_specs=[
            pl.BlockSpec((block, features), lambda i: (i, 0)),
            pl.BlockSpec((block, 1), lambda i: (i, 0)),
            pl.BlockSpec((block, 1), lambda i: (i, 0)),
            pl.BlockSpec((width, features), lambda i: (0, 0)),
            pl.BlockSpec((1, width), lambda i: (0, 0)),
            pl.BlockSpec((1, width), lambda i: (0, 0)),
        ],
        out_specs=pl.BlockSpec((block, width), lambda i: (i, 0)),
        compiler_params=pltpu.CompilerParams(vmem_limit_bytes=52 * MIB),
        cost_estimate=pl.CostEstimate(
            flops=8 * count * width * features, bytes_accessed=2 * count * width, transcendentals=count * width
        ),
        name="tile",
    )(points, point_squares[:, None], ids[:, None], chosen, panel_squares[None, :], panel[None, :])


def product_kernel(*refs):
    *tile_refs, here_ref, there_ref, out_ref = refs
    blocks = here_ref.shape[0]
    total = jnp.zeros(out_ref.shape, jnp.float32)
    for part, tile_ref in enumerate(tile_refs):
        update = here_ref[part] if part < blocks else there_ref[part - blocks]
        total = total + lax.dot_general(
            tile_ref[...], update, TRANSPOSED, preferred_element_type=jnp.float32
        )
    out_ref[...] = total


def product(tile, here, there, first, count):
    blocks, targets, width = here.shape
    line = 256
    skip = first // line
    panel = tile.shape[1]
    whole = pl.BlockSpec(here.shape, lambda i: (0, 0, 0))
    parts = [pl.BlockSpec((line, width), lambda i, part=part: (i + skip, part)) for part in range(2 * blocks)]
    return pl.pallas_call(
        product_kernel,
        grid=(count // line,),
        out_shape=jax.ShapeDtypeStruct((count, targets), jnp.float32),
        in_specs=[*parts, whole, whole],
        out_specs=pl.BlockSpec((line, targets), lambda i: (i, 0)),
        compiler_params=pltpu.CompilerParams(vmem_limit_bytes=52 * MIB),
        cost_estimate=pl.CostEstimate(
            flops=4 * count * panel * targets, bytes_accessed=2 * count * panel, transcendentals=0
        ),
        name="product",
    )(*[tile] * len(parts), here, there)


def finish_kernel(half_ref, rest_ref, out_ref):
    blocks, _, width = half_ref.shape
    for block in range(blocks):
        whole = half_ref[block].astype(jnp.float32) + rest_ref[block].astype(jnp.float32)
        out_ref[pl.ds(block * width, width), :] = whole.T


def finish(half, rest):
    blocks, targets, width = half.shape
    vmem = pl.BlockSpec(memory_space=pltpu.VMEM)
    return pl.pallas_call(
        finish_kernel,
        out_shape=jax.ShapeDtypeStruct((blocks * width, targets), jnp.float32),
        in_specs=[vmem] * 2,
        out_specs=vmem,
        compiler_params=pltpu.CompilerParams(vmem_limit_bytes=16 * MIB),
        cost_estimate=pl.CostEstimate(flops=10**6, bytes_accessed=2 * 10**6, transcendentals=0),
        name="finish",
    )(half, rest)


def shift(value, axis, by):
    size = lax.axis_size(axis)
    return lax.ppermute(value, axis, [(i, (i + by) % size) for i in range(size)])


def ring_gather(value, axis):
    half = value.shape[0] // 2
    before = shift(value, axis, 1)
    after = shift(value, axis, -1)
    top = shift(before[:half], axis, 1)
    bottom = shift(after[half:], axis, -1)
    return [value, after, jnp.concatenate([top, bottom], axis=0), before]


def on_device(points, gradient, panel_index):
    own, features = points.shape
    targets = gradient.shape[1]
    blocks, width = panel_index.shape
    shard = blocks * width
    rows, near, xs, ks = (lax.axis_size(name) for name in (ROWS, NEAR, "x", "k"))
    cols = xs * ks
    row, x, core = lax.axis_index(ROWS), lax.axis_index("x"), lax.axis_index("k")
    group_start = row * own * cols
    share = shard // near
    groups = targets // FEW

    tables = [panel_index] + [shift(panel_index, "x", by) for by in range(1, xs)]
    other_points = shift(points, "k", 1)
    other_grads = shift(gradient, "k", 1)
    own_share = lax.dynamic_index_in_dim(panel_index.reshape(near, share), row % near, 0, False)
    block = row // groups
    block_index = lax.dynamic_index_in_dim(panel_index, block, 0, False)
    start = (row * xs + x) * own * ks
    rounds, rank = ranks(tables, block_index)
    rounds = jnp.maximum(rounds, shift(rounds, "k", 1))

    def exchange(message):
        return lax.all_to_all(message, ROUTE, 0, 0)

    def exchange_by_axis(message):
        message = message.reshape(*(lax.axis_size(axis) for axis in ROUTE), SLOTS, 128)
        for dim, axis in enumerate(ROUTE):
            message = lax.all_to_all(message, axis, dim, dim, tiled=True)
        return message

    def route(number, exchange, unroll):
        scalars = jnp.stack([number, start, x, core]).astype(jnp.int32)
        message = pack(scalars, tables, points, other_points, gradient, other_grads, unroll).reshape(rows * xs, SLOTS, 128)
        message = exchange(message).reshape(rows * xs * SLOTS, 128)
        return place(scalars, message, own_share, block_index, rank, near, 8 if unroll else 1)

    def further(state):
        number, piece, right = state
        more_piece, more_right = route(number, exchange_by_axis, False)
        return number + 1, piece + more_piece, right + more_right

    piece, right_side = route(jnp.int32(0), exchange, True)
    last = rounds[0, 0]
    _, piece, right_side = lax.while_loop(
        lambda state: state[0] < last, further, (jnp.int32(1), piece, right_side)
    )
    chosen = lax.all_to_all(piece, NEAR, 0, 0).reshape(shard, features)

    own_block = lax.dynamic_index_in_dim(chosen.reshape(blocks, width, features), block, 0, False)
    half, rest = solve(own_block, right_side, rows)
    half = lax.all_to_all(half, ROWS, 0, 0).reshape(blocks, targets, width)

    calm_points, _ = lax.optimization_barrier((points, tables))
    mine, after, far, before = ring_gather(calm_points, "x")
    core_points = jnp.concatenate([far, after, before, mine])
    indices = panel_index.reshape(-1)
    both_chosen = jnp.concatenate([chosen, shift(chosen, "k", 1)])
    both_panel = jnp.concatenate([indices, shift(indices, "k", 1)])
    ahead = (x + jnp.array([2, 1, 3, 0], jnp.int32)) % xs
    ids = group_start + (ahead * ks + core)[:, None] * own + jnp.arange(own, dtype=jnp.int32)[None, :]
    tile = build_tile(core_points, ids.reshape(-1), both_chosen, both_panel)

    half, tile, rest = lax.optimization_barrier((half, tile, rest))
    rest = lax.all_to_all(rest, ROWS, 0, 0).reshape(blocks, targets, width)
    other = shift(half, "k", 1)

    far = product(tile, half, other, 0, own)
    near = product(tile, half, other, own, 2 * own)
    mine = product(tile, half, other, 3 * own, own)
    middle = own // 2
    top = shift(far[:middle], "x", 1)
    bottom = shift(far[middle:], "x", -1)
    send_after = jnp.concatenate([near[:middle] + top, near[middle:own]])
    send_before = jnp.concatenate([near[own : own + middle], near[own + middle :] + bottom])
    from_before = shift(send_after, "x", 1)
    from_after = shift(send_before, "x", -1)
    new_gradient = gradient + (mine + from_before + from_after)
    return new_gradient, finish(half, rest)


def solution(mesh):
    fine = Mesh(mesh.devices.reshape(4, 2, 4, 4, 2), DEVICES)
    in_specs = (P(DEVICES, None), P(DEVICES, None), P(("x", "k"), None))
    out_specs = (P(DEVICES, None), P(("x", "k"), None))
    return jax.shard_map(on_device, mesh=fine, in_specs=in_specs, out_specs=out_specs, check_vma=False)
```

```python
import functools

import jax
import jax.numpy as jnp
from jax import lax
from jax.experimental import pallas as pl
from jax.experimental.pallas import tpu as pltpu
from jax.sharding import Mesh
from jax.sharding import PartitionSpec as P

ITERS = 8
RIDGE = 1.0
LOG2E = 1.4426950408889634
DEVICES = ("zh", "zl", "y", "x", "k")
ROUTE = ("x", "zh", "zl", "y")
ROWS = ("zh", "zl", "y")
NEAR = ("zl", "y")
TRANSPOSED = (((1,), (1,)), ((), ()))
FIRST = (((0,), (0,)), ((), ()))
MIB = 1 << 20
POINT_SLOTS = 12
PIECES = 2
GRAD_SLOTS = 32
SLOTS = 16
FEW = 8
CHIPS = 128
XS = 4
OWN = 1024
SHARE = 256
NONE = 1 << 20


def iota(shape, axis):
    return lax.broadcasted_iota(jnp.int32, shape, axis)


def owner_place(index, own, xs, rows):
    chip = index // own
    return (chip % xs) * rows + chip // xs


def pack_kernel(
    scalar_ref, here_ref, one_ref, two_ref, three_ref, points_ref, other_points_ref, grads_ref, other_grads_ref,
    out_ref, values_ref, rows_ref, table_ref, *, unroll,
):
    tables = (here_ref, one_ref, two_ref, three_ref)
    per_shard, width = here_ref.shape
    each, targets = grads_ref.shape
    own = 2 * each
    groups = targets // FEW
    blocks = len(tables) * per_shard
    devices = blocks * groups
    share = width // groups
    per = 128 // FEW
    number = scalar_ref[0]
    for back, table in enumerate(tables):
        shard = (scalar_ref[2] - back) & (len(tables) - 1)
        for lane in range(0, width, 128):
            pair = table[:, lane : lane + 128]
            turned = pltpu.roll(pair, share, 1)
            for block in range(per_shard):
                line = (shard * per_shard + block) * groups + lane // share
                table_ref[pl.ds(line, 1), :] = pair[block : block + 1]
                table_ref[pl.ds(line + 1, 1), :] = turned[block : block + 1]
    offset = table_ref[:, :share] - scalar_ref[1]
    mine = (offset >= 0) & (offset < own)
    held = mine.astype(jnp.bfloat16)
    offset = jnp.where(scalar_ref[3] == 0, offset, jnp.where(offset < each, offset + each, offset - each))
    code = jnp.where(mine, (offset + 1).astype(jnp.float32), 0.0)
    upper = (iota((share, share), 0) < iota((share, share), 1)).astype(jnp.bfloat16)
    rank = jnp.dot(held, upper, preferred_element_type=jnp.float32)
    count = jnp.dot(held, jnp.ones((share, share), jnp.bfloat16), preferred_element_type=jnp.float32)
    left, right = iota((devices, devices), 0), iota((devices, devices), 1)
    earlier = ((left // groups == right // groups) & (right < left)).astype(jnp.bfloat16)
    before = jnp.dot(earlier, count.astype(jnp.bfloat16), preferred_element_type=jnp.float32)
    block_rank = rank + before
    span = SHARE // share
    earlier = ((left // span == right // span) & (right < left)).astype(jnp.bfloat16)
    rank = rank + jnp.dot(earlier, count.astype(jnp.bfloat16), preferred_element_type=jnp.float32)

    lanes = iota((devices, 128), 1)
    first = (number * POINT_SLOTS).astype(jnp.float32)
    found = jnp.zeros((devices, 128), jnp.float32)
    for slot in range(POINT_SLOTS):
        chosen = jnp.sum(jnp.where(rank == first + slot, code, 0.0), axis=1, keepdims=True)
        high = jnp.floor(chosen * 0.125)
        found = jnp.where(lanes == slot, high, jnp.where(lanes == slot + 64, chosen - 8.0 * high, found))
    lines = devices // len(tables)
    shares = lines // span
    reach = ((left // lines == right // lines) & (left % shares == right % lines // span)).astype(jnp.bfloat16)
    found = jnp.dot(reach, found.astype(jnp.bfloat16), preferred_element_type=jnp.float32)
    lanes = iota((devices, own), 1)
    for slot in range(POINT_SLOTS):
        chosen = 8.0 * found[:, slot : slot + 1] + found[:, slot + 64 : slot + 65]
        pick = (lanes + 1 == chosen.astype(jnp.int32)).astype(jnp.bfloat16)
        rows_ref[pl.ds(slot, devices, stride=SLOTS), :] = jnp.dot(
            pick[:, :each], points_ref[...], preferred_element_type=jnp.float32
        ) + jnp.dot(pick[:, each:], other_points_ref[...], preferred_element_type=jnp.float32)

    lanes = iota((devices, 128), 1)
    keep = iota((blocks, 128), 1) // per == iota((blocks, 128), 0)
    parts = []
    left = jnp.concatenate([grads_ref[...], other_grads_ref[...]], axis=0)
    for _ in range(PIECES):
        part = left.astype(jnp.bfloat16)
        left = left - part.astype(jnp.float32)
        parts.append(part)

    @pl.loop(0, GRAD_SLOTS // per, unroll=unroll)
    def _(turn):
        first = (number * GRAD_SLOTS + turn * per).astype(jnp.float32)
        found = jnp.zeros((devices, 128), jnp.float32)
        for slot in range(per):
            chosen = jnp.sum(jnp.where(block_rank == first + slot, code, 0.0), axis=1, keepdims=True)
            found = jnp.where(lanes % per == slot, chosen, found)
        found = jnp.sum(found.reshape(blocks, groups, 128), axis=1)
        found = jnp.sum(jnp.where(keep, found, 0.0), axis=0, keepdims=True).astype(jnp.int32)
        pick = (iota((own, 128), 0) + 1 == found).astype(jnp.bfloat16)
        values = jnp.zeros((targets, 128), jnp.float32)
        for part in parts:
            values = values + lax.dot_general(part, pick, FIRST, preferred_element_type=jnp.float32)
        values_ref[...] = values
        places = iota((groups, 128), 1) // per
        message = [jnp.zeros((groups, 128), jnp.float32) for _ in range(blocks)]
        for target in range(FEW):
            taken = values_ref[pl.ds(target, groups, stride=FEW), :]
            for block in range(blocks):
                by = (target - block) * per % 128
                turned = pltpu.roll(taken, by, 1) if by else taken
                message[block] = jnp.where(places == target, turned, message[block])
        rest = jnp.concatenate(message, axis=0)
        for place in range(PIECES):
            part = rest.astype(jnp.bfloat16).astype(jnp.float32)
            rest = rest - part
            rows_ref[pl.ds(POINT_SLOTS + PIECES * turn + place, devices, stride=SLOTS), :] = part

    out_ref[...] = rows_ref[...].astype(jnp.bfloat16)


def pack(scalars, tables, points, other_points, grads, other_grads, unroll):
    targets = grads.shape[1]
    devices = len(tables) * tables[0].shape[0] * targets // FEW
    vmem = pl.BlockSpec(memory_space=pltpu.VMEM)
    return pl.pallas_call(
        functools.partial(pack_kernel, unroll=unroll),
        out_shape=jax.ShapeDtypeStruct((devices * SLOTS, 128), jnp.bfloat16),
        in_specs=[pl.BlockSpec(memory_space=pltpu.SMEM)] + [vmem] * 8,
        out_specs=vmem,
        scratch_shapes=[
            pltpu.VMEM((targets, 128), jnp.float32),
            pltpu.VMEM((devices * SLOTS, 128), jnp.float32),
            pltpu.VMEM((devices, 128), jnp.int32),
        ],
        compiler_params=pltpu.CompilerParams(vmem_limit_bytes=16 * MIB),
        name="pack",
    )(scalars, *tables, points, other_points, grads, other_grads)


def ranks_kernel(here_ref, one_ref, two_ref, three_ref, block_row_ref, block_column_ref, rounds_ref, rank_ref):
    tables = (here_ref, one_ref, two_ref, three_ref)
    per_shard, width = here_ref.shape
    share = SHARE
    segments = iota((width, 128), 0) // share == iota((width, 128), 1)
    segments = segments | (iota((width, 128), 1) == 127)
    segments = segments.astype(jnp.bfloat16)
    most = jnp.zeros((CHIPS, 128), jnp.float32)
    chip = iota((CHIPS, width), 0)

    def count(block, most):
        for table in tables:
            hit = (chip == table[pl.ds(block, 1), :] // OWN).astype(jnp.bfloat16)
            most = jnp.maximum(most, jnp.dot(hit, segments, preferred_element_type=jnp.float32))
        return most

    most = lax.fori_loop(0, per_shard, count, most)
    whole = iota((CHIPS, 128), 1) == 127
    most_block = jnp.max(jnp.where(whole, most, 0.0), keepdims=True).astype(jnp.int32)
    most_share = jnp.max(jnp.where(whole, 0.0, most), keepdims=True).astype(jnp.int32)
    rounds_ref[...] = jnp.maximum(
        (most_block + GRAD_SLOTS - 1) // GRAD_SLOTS, (most_share + POINT_SLOTS - 1) // POINT_SLOTS
    )
    owners = block_row_ref[...] // OWN
    step = 128

    def compare(number, total):
        start = pl.multiple_of(number * step, step)
        others = block_column_ref[pl.ds(start, step), :] // OWN
        earlier = iota((step, width), 0) + start < iota((step, width), 1)
        same = jnp.where((others == owners) & earlier, 1, 0)
        return total + jnp.sum(same.reshape(step // 8, 8, width), axis=0)

    total = lax.fori_loop(0, width // step, compare, jnp.zeros((8, width), jnp.int32))
    rank_ref[...] = jnp.sum(total, axis=0, keepdims=True)


def ranks(tables, block_index):
    vmem = pl.BlockSpec(memory_space=pltpu.VMEM)
    width = block_index.shape[0]
    return pl.pallas_call(
        ranks_kernel,
        out_shape=(
            jax.ShapeDtypeStruct((1, 1), jnp.int32),
            jax.ShapeDtypeStruct((1, width), jnp.int32),
        ),
        in_specs=[vmem] * 6,
        out_specs=(vmem, vmem),
        compiler_params=pltpu.CompilerParams(vmem_limit_bytes=16 * MIB),
        cost_estimate=pl.CostEstimate(flops=4 * 10**9, bytes_accessed=10**5, transcendentals=0),
        name="ranks",
    )(*tables, block_index[None, :], block_index[:, None])


def place_kernel(scalar_ref, message_ref, row_ref, column_ref, block_ref, rank_ref, piece_ref, right_ref, *, unroll):
    length = message_ref.shape[0]
    share = column_ref.shape[0]
    width = block_ref.shape[1]
    per = 128 // FEW
    turns = GRAD_SLOTS // per
    number = scalar_ref[0]
    row_owner = owner_place(row_ref[...], OWN, XS, CHIPS // XS)
    column_owner = owner_place(column_ref[...], OWN, XS, CHIPS // XS)
    earlier = iota((share, share), 1) < iota((share, share), 0)
    rank = jnp.sum(
        jnp.where((row_owner == column_owner) & earlier, 1.0, 0.0), axis=1, keepdims=True
    ).astype(jnp.int32)
    slot = rank - number * POINT_SLOTS
    code = jnp.where((slot >= 0) & (slot < POINT_SLOTS), column_owner * SLOTS + slot, -1)
    slot = rank_ref[...] - number * GRAD_SLOTS
    wanted = owner_place(block_ref[...], OWN, XS, CHIPS // XS) * turns + slot // per
    wanted = jnp.where((slot >= 0) & (slot < GRAD_SLOTS), wanted, -NONE)
    step = 256
    def gather(number, state):
        found, piece = state
        start = pl.multiple_of(number * step, step)
        message = message_ref[pl.ds(start, step), :]
        line = iota((step, width), 0)
        turn = (line % SLOTS - POINT_SLOTS + PIECES) // PIECES - 1
        source = jnp.where((turn >= 0) & (turn < turns), line // SLOTS * turns + turn, 2 * NONE)
        pick = (source == wanted - number * (step // SLOTS * turns)).astype(jnp.bfloat16)
        found = found + lax.dot_general(message, pick, FIRST, preferred_element_type=jnp.float32)
        pick = (iota((share, step), 1) == code - start).astype(jnp.bfloat16)
        return found, piece + jnp.dot(pick, message, preferred_element_type=jnp.float32)

    state = jnp.zeros((128, width), jnp.float32), jnp.zeros((share, 128), jnp.float32)
    found, piece = lax.fori_loop(0, length // step, gather, state, unroll=unroll)
    piece = piece.astype(jnp.bfloat16)
    for copy in range(piece_ref.shape[0]):
        piece_ref[copy] = piece
    here = iota((per, width), 0) == slot % per
    for target in range(FEW):
        part = found[target * per : (target + 1) * per]
        right_ref[pl.ds(target, 1), :] = -jnp.sum(jnp.where(here, part, 0.0), axis=0, keepdims=True)


def place(scalars, message, index, block_index, rank, copies, unroll):
    vmem = pl.BlockSpec(memory_space=pltpu.VMEM)
    share, width = index.shape[0], block_index.shape[0]
    return pl.pallas_call(
        functools.partial(place_kernel, unroll=unroll),
        out_shape=(
            jax.ShapeDtypeStruct((copies, share, 128), jnp.bfloat16),
            jax.ShapeDtypeStruct((FEW, width), jnp.float32),
        ),
        in_specs=[pl.BlockSpec(memory_space=pltpu.SMEM)] + [vmem] * 5,
        out_specs=(vmem, vmem),
        compiler_params=pltpu.CompilerParams(vmem_limit_bytes=16 * MIB),
        name="place",
    )(scalars, message, index[None, :], index[:, None], block_index[None, :], rank)


def solve_kernel(points_ref, right_ref, half_ref, rest_ref, high_ref, low_ref):
    width = points_ref.shape[0]
    scale = -2.0 / points_ref.shape[1] * LOG2E
    step = 256
    same = iota((step, step), 0) == iota((step, step), 1)
    columns, lines = [], []
    for start in range(0, width, step):
        part = points_ref[pl.ds(start, step), :]
        inner = lax.dot_general(part, part, TRANSPOSED, preferred_element_type=jnp.float32)
        inner = jnp.where(same, inner, 0.0)
        columns.append(jnp.sum(inner, axis=1, keepdims=True))
        lines.append(jnp.sum(inner, axis=0, keepdims=True))
    line = jnp.concatenate(lines, axis=1)
    upper = jnp.zeros((1, 1), jnp.float32)
    for number, start in enumerate(range(0, width, step)):
        piece = pl.ds(start, step)
        inner = lax.dot_general(
            points_ref[piece, :], points_ref[...], TRANSPOSED, preferred_element_type=jnp.float32
        )
        distance = jnp.maximum(columns[number] + line - 2.0 * inner, 0.0)
        values = jnp.exp2(distance * scale)
        sums = jnp.sum(values, axis=1, keepdims=True)
        upper = jnp.maximum(upper, jnp.max(sums, axis=0, keepdims=True))
        high = values.astype(jnp.bfloat16)
        high_ref[piece, :] = high
        low_ref[piece, :] = (values - high.astype(jnp.float32)).astype(jnp.bfloat16)
    upper = upper + RIDGE
    center = (upper + RIDGE) / 2.0
    radius = (upper - RIDGE) / 2.0
    ratio = center / radius
    factor = 1.0 / ratio
    residual = right_ref[...]
    targets = residual.shape[0]
    direction = residual / center
    update = jnp.zeros_like(residual)
    for iteration in range(ITERS):
        update = update + direction
        if iteration < ITERS - 1:
            high = direction.astype(jnp.bfloat16)
            low = (direction - high.astype(jnp.float32)).astype(jnp.bfloat16)
            both = jnp.concatenate([high, low], axis=0)
            main = jnp.dot(both, high_ref[...], preferred_element_type=jnp.float32)
            rest = jnp.dot(high, low_ref[...], preferred_element_type=jnp.float32)
            product = main[:targets] + (main[targets:] + rest)
            residual = residual - (product + RIDGE * direction)
            following = 1.0 / (2.0 * ratio - factor)
            direction = following * factor * direction + 2.0 * following / radius * residual
            factor = following
    half = update.astype(jnp.bfloat16)
    rest = (update - half.astype(jnp.float32)).astype(jnp.bfloat16)
    for copy in range(half_ref.shape[0]):
        half_ref[copy] = half
        rest_ref[copy] = rest


def solve(points, right_side, copies):
    width, _ = points.shape
    vmem = pl.BlockSpec(memory_space=pltpu.VMEM)
    return pl.pallas_call(
        solve_kernel,
        out_shape=(jax.ShapeDtypeStruct((copies, *right_side.shape), jnp.bfloat16),) * 2,
        in_specs=[vmem] * 2,
        out_specs=(vmem, vmem),
        scratch_shapes=[pltpu.VMEM((width, width), jnp.bfloat16)] * 2,
        compiler_params=pltpu.CompilerParams(vmem_limit_bytes=16 * MIB),
        cost_estimate=pl.CostEstimate(flops=6 * 10**9, bytes_accessed=10**6, transcendentals=width * width),
        name="solve",
    )(points, right_side)


def tile_kernel(points_ref, column_ref, ids_ref, chosen_ref, row_ref, panel_ref, out_ref):
    scale = -2.0 / points_ref.shape[1] * LOG2E
    step = 512

    def part(number, _):
        piece = pl.ds(pl.multiple_of(number * step, step), step)
        inner = lax.dot_general(
            points_ref[...], chosen_ref[piece, :], TRANSPOSED, preferred_element_type=jnp.float32
        )
        distance = jnp.maximum(column_ref[...] + row_ref[:, piece] - 2.0 * inner, 0.0)
        values = jnp.exp2(distance * scale)
        values = jnp.where(ids_ref[...] == panel_ref[:, piece], values + RIDGE, values)
        out_ref[:, piece] = values.astype(jnp.bfloat16)
        return 0

    lax.fori_loop(0, chosen_ref.shape[0] // step, part, 0, unroll=4)


def build_tile(points, ids, chosen, panel):
    count, features = points.shape
    width = chosen.shape[0]
    block = 256
    point_squares = jnp.sum(jnp.square(points.astype(jnp.float32)), axis=-1)
    panel_squares = jnp.sum(jnp.square(chosen.astype(jnp.float32)), axis=-1)
    return pl.pallas_call(
        tile_kernel,
        grid=(count // block,),
        out_shape=jax.ShapeDtypeStruct((count, width), jnp.bfloat16),
        in_specs=[
            pl.BlockSpec((block, features), lambda i: (i, 0)),
            pl.BlockSpec((block, 1), lambda i: (i, 0)),
            pl.BlockSpec((block, 1), lambda i: (i, 0)),
            pl.BlockSpec((width, features), lambda i: (0, 0)),
            pl.BlockSpec((1, width), lambda i: (0, 0)),
            pl.BlockSpec((1, width), lambda i: (0, 0)),
        ],
        out_specs=pl.BlockSpec((block, width), lambda i: (i, 0)),
        compiler_params=pltpu.CompilerParams(vmem_limit_bytes=52 * MIB),
        cost_estimate=pl.CostEstimate(
            flops=8 * count * width * features, bytes_accessed=2 * count * width, transcendentals=count * width
        ),
        name="tile",
    )(points, point_squares[:, None], ids[:, None], chosen, panel_squares[None, :], panel[None, :])


def product_kernel(*refs):
    *tile_refs, here_ref, there_ref, out_ref = refs
    blocks = here_ref.shape[0]
    total = jnp.zeros(out_ref.shape, jnp.float32)
    for part, tile_ref in enumerate(tile_refs):
        update = here_ref[part] if part < blocks else there_ref[part - blocks]
        total = total + lax.dot_general(
            tile_ref[...], update, TRANSPOSED, preferred_element_type=jnp.float32
        )
    out_ref[...] = total


def product(tile, here, there, first, count):
    blocks, targets, width = here.shape
    line = 256
    skip = first // line
    panel = tile.shape[1]
    whole = pl.BlockSpec(here.shape, lambda i: (0, 0, 0))
    parts = [pl.BlockSpec((line, width), lambda i, part=part: (i + skip, part)) for part in range(2 * blocks)]
    return pl.pallas_call(
        product_kernel,
        grid=(count // line,),
        out_shape=jax.ShapeDtypeStruct((count, targets), jnp.float32),
        in_specs=[*parts, whole, whole],
        out_specs=pl.BlockSpec((line, targets), lambda i: (i, 0)),
        compiler_params=pltpu.CompilerParams(vmem_limit_bytes=52 * MIB),
        cost_estimate=pl.CostEstimate(
            flops=4 * count * panel * targets, bytes_accessed=2 * count * panel, transcendentals=0
        ),
        name="product",
    )(*[tile] * len(parts), here, there)


def finish_kernel(half_ref, rest_ref, out_ref):
    blocks, _, width = half_ref.shape
    for block in range(blocks):
        whole = half_ref[block].astype(jnp.float32) + rest_ref[block].astype(jnp.float32)
        out_ref[pl.ds(block * width, width), :] = whole.T


def finish(half, rest):
    blocks, targets, width = half.shape
    vmem = pl.BlockSpec(memory_space=pltpu.VMEM)
    return pl.pallas_call(
        finish_kernel,
        out_shape=jax.ShapeDtypeStruct((blocks * width, targets), jnp.float32),
        in_specs=[vmem] * 2,
        out_specs=vmem,
        compiler_params=pltpu.CompilerParams(vmem_limit_bytes=16 * MIB),
        cost_estimate=pl.CostEstimate(flops=10**6, bytes_accessed=2 * 10**6, transcendentals=0),
        name="finish",
    )(half, rest)


def shift(value, axis, by):
    size = lax.axis_size(axis)
    return lax.ppermute(value, axis, [(i, (i + by) % size) for i in range(size)])


def ring_gather(value, axis):
    half = value.shape[0] // 2
    before = shift(value, axis, 1)
    after = shift(value, axis, -1)
    top = shift(before[:half], axis, 1)
    bottom = shift(after[half:], axis, -1)
    return [value, after, jnp.concatenate([top, bottom], axis=0), before]


def on_device(points, gradient, panel_index):
    own, features = points.shape
    targets = gradient.shape[1]
    blocks, width = panel_index.shape
    shard = blocks * width
    rows, near, xs, ks = (lax.axis_size(name) for name in (ROWS, NEAR, "x", "k"))
    cols = xs * ks
    row, x, core = lax.axis_index(ROWS), lax.axis_index("x"), lax.axis_index("k")
    group_start = row * own * cols
    share = shard // near
    groups = targets // FEW

    tables = [panel_index] + [shift(panel_index, "x", by) for by in range(1, xs)]
    other_points = shift(points, "k", 1)
    other_grads = shift(gradient, "k", 1)
    own_share = lax.dynamic_index_in_dim(panel_index.reshape(near, share), row % near, 0, False)
    block = row // groups
    block_index = lax.dynamic_index_in_dim(panel_index, block, 0, False)
    start = (row * xs + x) * own * ks
    rounds, rank = ranks(tables, block_index)
    rounds = jnp.maximum(rounds, shift(rounds, "k", 1))

    def exchange(message):
        return lax.all_to_all(message, ROUTE, 0, 0)

    def exchange_by_axis(message):
        message = message.reshape(*(lax.axis_size(axis) for axis in ROUTE), SLOTS, 128)
        for dim, axis in enumerate(ROUTE):
            message = lax.all_to_all(message, axis, dim, dim, tiled=True)
        return message

    def route(number, exchange, unroll):
        scalars = jnp.stack([number, start, x, core]).astype(jnp.int32)
        message = pack(scalars, tables, points, other_points, gradient, other_grads, unroll).reshape(rows * xs, SLOTS, 128)
        message = exchange(message).reshape(rows * xs * SLOTS, 128)
        return place(scalars, message, own_share, block_index, rank, near, 8 if unroll else 1)

    def further(state):
        number, piece, right = state
        more_piece, more_right = route(number, exchange_by_axis, False)
        return number + 1, piece + more_piece, right + more_right

    piece, right_side = route(jnp.int32(0), exchange, True)
    last = rounds[0, 0]
    _, piece, right_side = lax.while_loop(
        lambda state: state[0] < last, further, (jnp.int32(1), piece, right_side)
    )
    chosen = lax.all_to_all(piece, NEAR, 0, 0).reshape(shard, features)

    own_block = lax.dynamic_index_in_dim(chosen.reshape(blocks, width, features), block, 0, False)
    half, rest = solve(own_block, right_side, rows)
    half = lax.all_to_all(half, ROWS, 0, 0).reshape(blocks, targets, width)

    calm_points, _ = lax.optimization_barrier((points, tables))
    mine, after, far, before = ring_gather(calm_points, "x")
    core_points = jnp.concatenate([far, after, before, mine])
    indices = panel_index.reshape(-1)
    both_chosen = jnp.concatenate([chosen, shift(chosen, "k", 1)])
    both_panel = jnp.concatenate([indices, shift(indices, "k", 1)])
    ahead = (x + jnp.array([2, 1, 3, 0], jnp.int32)) % xs
    ids = group_start + (ahead * ks + core)[:, None] * own + jnp.arange(own, dtype=jnp.int32)[None, :]
    tile = build_tile(core_points, ids.reshape(-1), both_chosen, both_panel)

    half, tile, rest = lax.optimization_barrier((half, tile, rest))
    rest = lax.all_to_all(rest, ROWS, 0, 0).reshape(blocks, targets, width)
    other = shift(half, "k", 1)

    far = product(tile, half, other, 0, own)
    near = product(tile, half, other, own, 2 * own)
    mine = product(tile, half, other, 3 * own, own)
    middle = own // 2
    top = shift(far[:middle], "x", 1)
    bottom = shift(far[middle:], "x", -1)
    send_after = jnp.concatenate([near[:middle] + top, near[middle:own]])
    send_before = jnp.concatenate([near[own : own + middle], near[own + middle :] + bottom])
    from_before = shift(send_after, "x", 1)
    from_after = shift(send_before, "x", -1)
    update = finish(half, rest)
    from_before, from_after, update = lax.optimization_barrier((from_before, from_after, update))
    return gradient + (mine + from_before + from_after), update


def solution(mesh):
    fine = Mesh(mesh.devices.reshape(4, 2, 4, 4, 2), DEVICES)
    in_specs = (P(DEVICES, None), P(DEVICES, None), P(("x", "k"), None))
    out_specs = (P(DEVICES, None), P(("x", "k"), None))
    return jax.shard_map(on_device, mesh=fine, in_specs=in_specs, out_specs=out_specs, check_vma=False)
```
